512 devices in a mesh: sec: 16 (over z_lo, y), xs: 32 (over z_hi, x, core).
Axes of the slice: x: 4, y: 8, z: 8 (z_hi: 4, z_lo: 2; z = z_hi * 2 + z_lo), core: 2. Of those that a mesh axis runs over, the one named last changes fastest.
Arguments:
- soot: float32 [96, 512, 1024], P('sec', 'xs'), may hold values from 0.05 to 1
- species: float32 [40, 512, 1024], P(None, 'xs'), may hold values from 0.1 to 1
- kernel: float32 [96, 96], replicated, may hold values from 0.002 to 0.02
- split: float32 [96, 96], replicated, may hold values from 0.2 to 0.8
- target: int32 [96, 96], replicated, may hold values from 0 to 94, as said below
- growth: float32 [96], replicated, may hold values from 0.05 to 0.5
- diffusivity: float32 [40], replicated, may hold values from 0.05 to 0.2
- reaction: float32 [40, 40], replicated, may hold values from -1 to 1
- stoich: float32 [40], replicated, may hold values from -1 to 1
Outputs:
- soot_out: float32 [96, 512, 1024], P('sec', 'xs')
- species_out: float32 [40, 512, 1024], P(None, 'xs')
The draws below stay inside these ranges and needn't reach their ends.
Inputs may be any that keep to these rules, and one draw needn't show every extreme that they name: target[i, j] = min(max(i, j) + r, 94) with r of 0 to 3.
All inputs are finite; a program needn't handle non-finite values.
Results may differ from the reference program's by a relative error of at most 0.0003.
Values sent between devices are 32-bit elements; how exact they have to be, the bound alone decides.
A program may use at most 128 MiB of HBM per device.

```python
import math
import jax
import jax.numpy as jnp
from jax import lax

S = 96
K = 40
CZ = 1024
NY = 512


def draw_target(key, part):
    rows = jnp.arange(S, dtype=jnp.int32)
    larger = jnp.maximum(rows[:, None], rows[None, :])
    offset = jax.random.randint(key, (S, S), 0, 4, dtype=jnp.int32)
    return jnp.minimum(larger + offset, S - 2).astype(jnp.int32)


def shard_levels(stream_key, dims, shards, smallest, largest):
    level = 1.0
    for axis_at, shards_of in shards:
        steps = jax.random.uniform(jax.random.fold_in(jax.random.fold_in(stream_key, 6), axis_at), (shards_of,), jnp.float32, smallest / len(shards), largest / len(shards))
        level = level * jnp.repeat(jnp.exp(steps), dims[axis_at] // shards_of).reshape((-1,) + (1,) * (len(dims) - 1 - axis_at))
    return level


def normal_values(own_key, extent, spread, limit, held_as=jnp.bfloat16):
    return jnp.clip(spread * jax.random.normal(own_key, extent, jnp.float32), -limit, limit).astype(held_as)


def setup_inputs(seed: int = 0) -> dict:
    key_list = jax.random.split(jax.random.key(seed), 10)
    return {
        "soot": jnp.clip(jnp.exp(math.log(1.0) - 2.9957323 * jax.random.uniform(key_list[0], (S, NY, CZ), jnp.float32) ** shard_levels(key_list[0], (S, NY, CZ), ((0, 16), (1, 32)), -0.2, 0.2)), 0.05, 1.0),
        "species": jnp.clip(jnp.exp(math.log(1.0) - 2.3025851 * jax.random.uniform(key_list[1], (K, NY, CZ), jnp.float32) ** shard_levels(key_list[1], (K, NY, CZ), ((1, 32),), -0.2, 0.2)), 0.1, 1.0),
        "kernel": jnp.clip(jnp.exp(jax.random.uniform(key_list[2], (S, S), jnp.float32, math.log(0.002), math.log(0.02))), 0.002, 0.02),
        "split": jnp.clip(jax.random.uniform(key_list[3], (S, S), jnp.float32, 0.2, 0.8), 0.2, 0.8),
        "target": draw_target(jax.random.fold_in(key_list[9], 71), 0),
        "growth": jnp.clip(jnp.exp(jax.random.uniform(key_list[5], (S,), jnp.float32, math.log(0.05), math.log(0.5))), 0.05, 0.5),
        "diffusivity": jnp.clip(jax.random.uniform(key_list[6], (K,), jnp.float32, 0.05, 0.2), 0.05, 0.2),
        "reaction": normal_values(key_list[7], (K, K), K ** -0.5, 1.0, jnp.float32),
        "stoich": jnp.clip(jax.random.uniform(key_list[8], (K,), jnp.float32, -1.0, 1.0), -1.0, 1.0),
    }


HI = lax.Precision.HIGHEST


def laplace(field):
    padded = jnp.pad(field, ((0, 0), (1, 1), (1, 1)))
    beside = padded[:, 2:, 1:-1] + padded[:, :-2, 1:-1] + padded[:, 1:-1, 2:] + padded[:, 1:-1, :-2]
    return beside - 4.0 * field


def birth_rows(dense, kernel, split, target, first, count):
    def one_target(index):
        weights = 0.5 * kernel * (split * (target == index).astype(kernel.dtype) + (1.0 - split) * (target + 1 == index).astype(kernel.dtype))
        product = jnp.dot(weights, dense, precision=HI)
        return jnp.sum(dense * product, axis=0)
    indices = (first + jnp.arange(count)).astype(jnp.int32)
    return lax.map(one_target, indices)


def reference(soot, species, kernel, split, target, growth, diffusivity, reaction, stoich):
    cells = soot.shape[1] * soot.shape[2]
    dense = soot.reshape(S, cells)
    acet = species[0].reshape(1, cells)
    birth = birth_rows(dense, kernel, split, target, 0, S)
    loss = dense * jnp.dot(kernel, dense, precision=HI)
    flux = growth[:, None] * dense * acet
    inflow = jnp.concatenate([jnp.zeros((1, cells), dense.dtype), flux[:-1]], axis=0)
    consumption = jnp.sum(flux, axis=0)
    rate = (birth - loss - flux + inflow).reshape(soot.shape)
    soot_out = soot + 0.1 * laplace(soot) + rate
    mixed = jnp.dot(reaction, species.reshape(K, cells), precision=HI).reshape(species.shape)
    species_out = species + diffusivity[:, None, None] * laplace(species) + mixed - stoich[:, None, None] * consumption.reshape(1, soot.shape[1], soot.shape[2])
    return soot_out, species_out
```

```python
import functools

import jax
import jax.numpy as jnp
from jax import lax
from jax.experimental import pallas as pl
from jax.experimental.pallas import tpu as pltpu
from jax.sharding import PartitionSpec as P

MESH = pl.DeviceIdType.MESH
F32, BF16 = jnp.float32, jnp.bfloat16
PAD = 8
LOW, HIGH = -1, 4
SLOTS = HIGH - LOW + 1


def split_bf16(x):
    high = x.astype(BF16)
    return high, (x - high.astype(F32)).astype(BF16)


def kernel(
    nsec, nxs, own, kinds,
    soot, species, kern, split, target, growth, diffusivity, reaction, stoich,
    soot_out, species_out,
    fields, result, dense, rate, used, rate_in, used_in,
    edge_out, edge_in, kern_v, split_v, target_v, growth_v, diff_v, react_v,
    react_pad, weights, lhs,
    load_sem, send_sem, recv_sem, back_send, back_recv, used_send, used_recv, edge_send, edge_recv,
):
    sections = nsec * own
    count = fields.shape[1]
    rows = fields.shape[2]
    blocks = fields.shape[0]
    width = blocks * 128
    me = lax.axis_index("sec")
    at = lax.axis_index("xs")
    before, after = (at + nxs - 1) % nxs, (at + 1) % nxs

    barrier = pltpu.get_barrier_semaphore()
    for step in range(1, nsec):
        pl.semaphore_signal(barrier, inc=1, device_id={"sec": (me + step) % nsec}, device_id_type=MESH)
    for neighbour in (before, after):
        pl.semaphore_signal(barrier, inc=1, device_id={"xs": neighbour}, device_id_type=MESH)

    def tile_rows(p):
        return pl.ds(pl.multiple_of((p // blocks) * 8, 8), 8)

    def tile_of(ref, p):
        return ref.at[:, tile_rows(p), pl.ds(pl.multiple_of((p % blocks) * 128, 128), 128)]

    loads = [pltpu.make_async_copy(tile_of(soot, me), dense.at[pl.ds(PAD + own * me, own)], load_sem.at[0])]
    for b in range(blocks):
        lanes = pl.ds(b * 128, 128)
        loads.append(pltpu.make_async_copy(species.at[:, :, lanes], fields.at[b, pl.ds(0, kinds)], load_sem.at[1 + b]))
        loads.append(pltpu.make_async_copy(soot.at[:, :, lanes], fields.at[b, pl.ds(kinds, own)], load_sem.at[1 + blocks + b]))
    tables = [(kern, kern_v), (split, split_v), (target, target_v), (growth, growth_v), (diffusivity, diff_v), (reaction, react_v)]
    for n, (src, dst) in enumerate(tables):
        loads.append(pltpu.make_async_copy(src, dst, load_sem.at[1 + 2 * blocks + n]))
    for copy in loads:
        copy.start()

    pl.semaphore_wait(barrier, nsec + 1)

    def sent(p, step):
        return pltpu.make_async_remote_copy(
            src_ref=tile_of(soot, p), dst_ref=dense.at[pl.ds(PAD + own * me, own)],
            send_sem=send_sem.at[step], recv_sem=recv_sem.at[me],
            device_id={"sec": p}, device_id_type=MESH)

    def got(p, step):
        return pltpu.make_async_remote_copy(
            src_ref=tile_of(soot, p), dst_ref=dense.at[pl.ds(PAD + own * p, own)],
            send_sem=send_sem.at[step], recv_sem=recv_sem.at[p],
            device_id={"sec": p}, device_id_type=MESH)

    for step in range(1, nsec):
        sent((me + step) % nsec, step).start()

    zero_tiles = jnp.zeros((PAD, 8, 128), F32)
    dense[0:PAD] = zero_tiles
    dense[PAD + sections:] = zero_tiles
    fields[:, kinds + own:] = jnp.zeros((blocks, count - kinds - own, rows, 128), F32)
    for copy in loads:
        copy.wait()

    flat = fields.reshape(blocks, count * rows, 128)
    flat_result = result.reshape(blocks, count * rows, 128)

    def row_of(r):
        return jnp.concatenate([flat[b, pl.ds(r, count, stride=rows), :] for b in range(blocks)], axis=1)

    edge_out[0] = row_of(0)
    edge_out[1] = row_of(rows - 1)

    def edge(side):
        return pltpu.make_async_remote_copy(
            src_ref=edge_out.at[side], dst_ref=edge_in.at[side],
            send_sem=edge_send.at[side], recv_sem=edge_recv.at[side],
            device_id={"xs": before if side == 0 else after}, device_id_type=MESH)

    edge(0).start()
    edge(1).start()

    i = lax.broadcasted_iota(jnp.int32, (sections, sections), 0)
    j = lax.broadcasted_iota(jnp.int32, (sections, sections), 1)
    rates = kern_v[...]
    shares = split_v[...]
    goal = target_v[...]
    low = 0.5 * rates * shares
    high = 0.5 * rates * (1.0 - shares)
    low_t, high_t, goal_t = low.T, high.T, goal.T
    weights[...] = jnp.zeros(weights.shape, F32)
    for slot in range(SLOTS):
        t = slot + LOW
        lower = jnp.where(goal == i + t, low, 0.0) + jnp.where(goal == i + (t - 1), high, 0.0)
        upper = jnp.where(goal_t == i + t, low_t, 0.0) + jnp.where(goal_t == i + (t - 1), high_t, 0.0)
        value = jnp.where(j <= i, lower, 0.0) + jnp.where(j < i, upper, 0.0)
        if t == 0:
            value = value - rates
        weights[slot, PAD + t:PAD + t + sections, 0:sections] = value
    for slot in range(SLOTS):
        top, rest = split_bf16(weights[slot, PAD:PAD + sections, :])
        here = pl.ds(slot * sections, sections)
        lhs[here, 0:128] = top
        lhs[here, 128:256] = top
        lhs[here, 256:384] = rest
    grow = growth_v[...].reshape(1, sections)
    grow_col = jnp.sum(jnp.where(i == j, grow, 0.0), axis=1, keepdims=True)
    grow_prev = jnp.sum(jnp.where(i == j + 1, grow, 0.0), axis=1, keepdims=True)

    fi = lax.broadcasted_iota(jnp.int32, (count, kinds), 0)
    fj = lax.broadcasted_iota(jnp.int32, (count, kinds), 1)
    diff_col = jnp.sum(jnp.where(fi == fj, diff_v[...].reshape(1, kinds), 0.0), axis=1, keepdims=True)
    fc = lax.broadcasted_iota(jnp.int32, (count, 1), 0)
    diff_col = diff_col + jnp.where((fc >= kinds) & (fc < kinds + own), 0.1, 0.0)
    react_pad[...] = jnp.zeros(react_pad.shape, F32)
    react_pad[0:kinds, 0:kinds] = react_v[...]
    mix = react_pad[...]
    mix_top = mix.astype(BF16).astype(F32)
    mix_rest = mix - mix_top
    mix_lhs = (mix_top + pltpu.roll(mix_top, kinds, 1) + pltpu.roll(mix_rest, 2 * kinds, 1)).astype(BF16)
    lane = lax.broadcasted_iota(jnp.int32, (count, width), 1)
    spare = jnp.zeros((128 - 3 * kinds, width), F32)

    def row_step(r, up, down):
        x = row_of(r)
        left = jnp.where(lane == 0, 0.0, pltpu.roll(x, 1, 1))
        right = jnp.where(lane == width - 1, 0.0, pltpu.roll(x, width - 1, 1))
        part = x[0:kinds]
        top = part.astype(BF16).astype(F32)
        rhs = jnp.concatenate([top, part - top, top, spare], axis=0).astype(BF16)
        mixed = jnp.dot(mix_lhs, rhs, preferred_element_type=F32)
        value = x + diff_col * (up + down + left + right - 4.0 * x) + mixed
        for b in range(blocks):
            flat_result[b, pl.ds(r, count, stride=rows), :] = value[:, b * 128:(b + 1) * 128]

    def inner(r, carry):
        row_step(r, row_of(r - 1), row_of(r + 1))
        return carry

    half = rows // 2
    lax.fori_loop(1, half, inner, 0)

    for step in range(1, nsec):
        got((me + step) % nsec, step).wait_recv()

    flat_dense = dense.reshape((sections + 2 * PAD) * 8, 128)
    flat_rate = rate.reshape(sections * 8, 128)
    acet = fields[me % blocks, 0, tile_rows(me), :]
    gap = jnp.zeros((128 - sections, 256), BF16)
    for pair in range(4):
        r0, r1 = 2 * pair, 2 * pair + 1

        def moved(t):
            start = 8 * (PAD - t)
            return jnp.concatenate(
                [flat_dense[pl.ds(start + r, sections, stride=8), :] for r in (r0, r1)], axis=1)

        held = moved(0)
        top, rest = split_bf16(held)
        rhs = jnp.concatenate([top, gap, rest, gap], axis=0)
        product = jnp.dot(lhs[:, 0:256], rhs, preferred_element_type=F32)
        product = product + jnp.dot(lhs[:, 256:384], rhs[0:128], preferred_element_type=F32)
        total = jnp.zeros((sections, 256), F32)
        for slot in range(SLOTS):
            total = total + moved(slot + LOW) * product[slot * sections:(slot + 1) * sections]
        growing = jnp.concatenate([acet[r0:r0 + 1], acet[r1:r1 + 1]], axis=1)
        flux = grow_col * held * growing
        total = total - flux + grow_prev * moved(1) * growing
        eaten = jnp.sum(flux, axis=0, keepdims=True)
        for n, r in enumerate((r0, r1)):
            flat_rate[pl.ds(r, sections, stride=8), :] = total[:, n * 128:(n + 1) * 128]
            used[r:r + 1, :] = eaten[:, n * 128:(n + 1) * 128]

    def rate_copy(p, source, step):
        return pltpu.make_async_remote_copy(
            src_ref=rate.at[pl.ds(own * p, own)], dst_ref=rate_in.at[source % blocks, :, tile_rows(source), :],
            send_sem=back_send.at[step], recv_sem=back_recv.at[source],
            device_id={"sec": p}, device_id_type=MESH)

    def used_copy(p, source, step):
        return pltpu.make_async_remote_copy(
            src_ref=used, dst_ref=used_in.at[source % blocks, tile_rows(source), :],
            send_sem=used_send.at[step], recv_sem=used_recv.at[source],
            device_id={"sec": p}, device_id_type=MESH)

    for step in range(1, nsec):
        p = (me + step) % nsec
        rate_copy(p, me, step).start()
        used_copy(p, me, step).start()
    rate_in[me % blocks, :, tile_rows(me), :] = rate[pl.ds(own * me, own)]
    used_in[me % blocks, tile_rows(me), :] = used[...]

    lax.fori_loop(half, rows - 1, inner, 0)
    edge(0).wait()
    edge(1).wait()
    row_step(0, jnp.where(at == 0, 0.0, edge_in[1]), row_of(1))
    row_step(rows - 1, row_of(rows - 2), jnp.where(at == nxs - 1, 0.0, edge_in[0]))

    for step in range(1, nsec):
        p = (me + step) % nsec
        rate_copy(p, p, step).wait_recv()
        used_copy(p, p, step).wait_recv()

    result[:, kinds:kinds + own] = result[:, kinds:kinds + own] + rate_in[...]

    def consume(s, carry):
        result[:, s] = result[:, s] - stoich[s] * used_in[...]
        return carry

    lax.fori_loop(0, kinds, consume, 0)

    stores = []
    for b in range(blocks):
        lanes = pl.ds(b * 128, 128)
        stores.append(pltpu.make_async_copy(result.at[b, pl.ds(0, kinds)], species_out.at[:, :, lanes], load_sem.at[1 + b]))
        stores.append(pltpu.make_async_copy(result.at[b, pl.ds(kinds, own)], soot_out.at[:, :, lanes], load_sem.at[1 + blocks + b]))
    for copy in stores:
        copy.start()
    for step in range(1, nsec):
        p = (me + step) % nsec
        sent(p, step).wait_send()
        rate_copy(p, me, step).wait_send()
        used_copy(p, me, step).wait_send()
    for copy in stores:
        copy.wait()


def shards(soot, species, kern, split, target, growth, diffusivity, reaction, stoich):
    own, rows, width = soot.shape
    kinds = species.shape[0]
    nsec, nxs = lax.axis_size("sec"), lax.axis_size("xs")
    sections = nsec * own
    blocks = width // 128
    count = -(-(kinds + own) // 8) * 8
    assert blocks * (rows // 8) == nsec and sections <= 128 and 3 * kinds <= 128
    dma = pltpu.SemaphoreType.DMA
    hbm = pl.BlockSpec(memory_space=pl.ANY)
    return pl.pallas_call(
        functools.partial(kernel, nsec, nxs, own, kinds),
        out_shape=(jax.ShapeDtypeStruct(soot.shape, F32), jax.ShapeDtypeStruct(species.shape, F32)),
        in_specs=[hbm] * 8 + [pl.BlockSpec(memory_space=pltpu.SMEM)],
        out_specs=(hbm, hbm),
        scratch_shapes=[
            pltpu.VMEM((blocks, count, rows, 128), F32),
            pltpu.VMEM((blocks, count, rows, 128), F32),
            pltpu.VMEM((sections + 2 * PAD, 8, 128), F32),
            pltpu.VMEM((sections, 8, 128), F32),
            pltpu.VMEM((8, 128), F32),
            pltpu.VMEM((blocks, own, rows, 128), F32),
            pltpu.VMEM((blocks, rows, 128), F32),
            pltpu.VMEM((2, count, width), F32),
            pltpu.VMEM((2, count, width), F32),
            pltpu.VMEM(kern.shape, F32),
            pltpu.VMEM(split.shape, F32),
            pltpu.VMEM(target.shape, jnp.int32),
            pltpu.VMEM(growth.shape, F32),
            pltpu.VMEM(diffusivity.shape, F32),
            pltpu.VMEM(reaction.shape, F32),
            pltpu.VMEM((count, 128), F32),
            pltpu.VMEM((SLOTS, sections + 2 * PAD, 128), F32),
            pltpu.VMEM((SLOTS * sections, 384), BF16),
            dma((1 + 2 * blocks + 6,)),
            dma((nsec,)), dma((nsec,)), dma((nsec,)), dma((nsec,)), dma((nsec,)), dma((nsec,)),
            dma((2,)), dma((2,)),
        ],
        compiler_params=pltpu.CompilerParams(
            collective_id=0, has_side_effects=True, vmem_limit_bytes=32 << 20),
    )(soot, species, kern, split, target, growth, diffusivity, reaction, stoich)


def solution(mesh):
    return jax.shard_map(
        shards,
        mesh=mesh,
        in_specs=(P("sec", "xs", None), P(None, "xs", None), P(), P(), P(), P(), P(), P(), P()),
        out_specs=(P("sec", "xs", None), P(None, "xs", None)),
        check_vma=False,
    )
```

```python
import functools

import jax
import jax.numpy as jnp
from jax import lax
from jax.experimental import pallas as pl
from jax.experimental.pallas import tpu as pltpu
from jax.sharding import PartitionSpec as P

MESH = pl.DeviceIdType.MESH
F32, BF16 = jnp.float32, jnp.bfloat16
PAD = 8
LOW, HIGH = -1, 4
SLOTS = HIGH - LOW + 1


def split_bf16(x):
    high = x.astype(BF16)
    return high, (x - high.astype(F32)).astype(BF16)


def kernel(
    nsec, nxs, own, kinds,
    soot, species, kern, split, target, growth, diffusivity, reaction,
    result, rate_in, used_in,
    fields, dense, rate, used,
    edge_out, edge_in, kern_v, split_v, target_v, growth_v, diff_v, react_v,
    react_pad, weights, lhs,
    load_sem, send_sem, recv_sem, back_send, back_recv, used_send, used_recv, edge_send, edge_recv,
):
    sections = nsec * own
    count = fields.shape[1]
    rows = fields.shape[2]
    blocks = fields.shape[0]
    width = blocks * 128
    me = lax.axis_index("sec")
    at = lax.axis_index("xs")
    before, after = (at + nxs - 1) % nxs, (at + 1) % nxs

    barrier = pltpu.get_barrier_semaphore()
    for step in range(1, nsec):
        pl.semaphore_signal(barrier, inc=1, device_id={"sec": (me + step) % nsec}, device_id_type=MESH)
    for neighbour in (before, after):
        pl.semaphore_signal(barrier, inc=1, device_id={"xs": neighbour}, device_id_type=MESH)

    def tile_rows(p):
        return pl.ds(pl.multiple_of((p // blocks) * 8, 8), 8)

    def tile_of(ref, p):
        return ref.at[:, tile_rows(p), pl.ds(pl.multiple_of((p % blocks) * 128, 128), 128)]

    loads = [pltpu.make_async_copy(tile_of(soot, me), dense.at[pl.ds(PAD + own * me, own)], load_sem.at[0])]
    for b in range(blocks):
        lanes = pl.ds(b * 128, 128)
        loads.append(pltpu.make_async_copy(species.at[:, :, lanes], fields.at[b, pl.ds(0, kinds)], load_sem.at[1 + b]))
        loads.append(pltpu.make_async_copy(soot.at[:, :, lanes], fields.at[b, pl.ds(kinds, own)], load_sem.at[1 + blocks + b]))
    tables = [(kern, kern_v), (split, split_v), (target, target_v), (growth, growth_v), (diffusivity, diff_v), (reaction, react_v)]
    for n, (src, dst) in enumerate(tables):
        loads.append(pltpu.make_async_copy(src, dst, load_sem.at[1 + 2 * blocks + n]))
    for copy in loads:
        copy.start()

    pl.semaphore_wait(barrier, nsec + 1)

    def sent(p, step):
        return pltpu.make_async_remote_copy(
            src_ref=tile_of(soot, p), dst_ref=dense.at[pl.ds(PAD + own * me, own)],
            send_sem=send_sem.at[step], recv_sem=recv_sem.at[me],
            device_id={"sec": p}, device_id_type=MESH)

    def got(p, step):
        return pltpu.make_async_remote_copy(
            src_ref=tile_of(soot, p), dst_ref=dense.at[pl.ds(PAD + own * p, own)],
            send_sem=send_sem.at[step], recv_sem=recv_sem.at[p],
            device_id={"sec": p}, device_id_type=MESH)

    for step in range(1, nsec):
        sent((me + step) % nsec, step).start()

    zero_tiles = jnp.zeros((PAD, 8, 128), F32)
    dense[0:PAD] = zero_tiles
    dense[PAD + sections:] = zero_tiles
    fields[:, kinds + own:] = jnp.zeros((blocks, count - kinds - own, rows, 128), F32)
    for copy in loads:
        copy.wait()

    flat = fields.reshape(blocks, count * rows, 128)
    flat_result = result.reshape(blocks, count * rows, 128)

    def row_of(r):
        return jnp.concatenate([flat[b, pl.ds(r, count, stride=rows), :] for b in range(blocks)], axis=1)

    edge_out[0] = row_of(0)
    edge_out[1] = row_of(rows - 1)

    def edge(side):
        return pltpu.make_async_remote_copy(
            src_ref=edge_out.at[side], dst_ref=edge_in.at[side],
            send_sem=edge_send.at[side], recv_sem=edge_recv.at[side],
            device_id={"xs": before if side == 0 else after}, device_id_type=MESH)

    edge(0).start()
    edge(1).start()

    i = lax.broadcasted_iota(jnp.int32, (sections, sections), 0)
    j = lax.broadcasted_iota(jnp.int32, (sections, sections), 1)
    rates = kern_v[...]
    shares = split_v[...]
    goal = target_v[...]
    low = 0.5 * rates * shares
    high = 0.5 * rates * (1.0 - shares)
    low_t, high_t, goal_t = low.T, high.T, goal.T
    weights[...] = jnp.zeros(weights.shape, F32)
    for slot in range(SLOTS):
        t = slot + LOW
        lower = jnp.where(goal == i + t, low, 0.0) + jnp.where(goal == i + (t - 1), high, 0.0)
        upper = jnp.where(goal_t == i + t, low_t, 0.0) + jnp.where(goal_t == i + (t - 1), high_t, 0.0)
        value = jnp.where(j <= i, lower, 0.0) + jnp.where(j < i, upper, 0.0)
        if t == 0:
            value = value - rates
        weights[slot, PAD + t:PAD + t + sections, 0:sections] = value
    for slot in range(SLOTS):
        top, rest = split_bf16(weights[slot, PAD:PAD + sections, :])
        here = pl.ds(slot * sections, sections)
        lhs[here, 0:128] = top
        lhs[here, 128:256] = top
        lhs[here, 256:384] = rest
    grow = growth_v[...].reshape(1, sections)
    grow_col = jnp.sum(jnp.where(i == j, grow, 0.0), axis=1, keepdims=True)
    grow_prev = jnp.sum(jnp.where(i == j + 1, grow, 0.0), axis=1, keepdims=True)

    fi = lax.broadcasted_iota(jnp.int32, (count, kinds), 0)
    fj = lax.broadcasted_iota(jnp.int32, (count, kinds), 1)
    diff_col = jnp.sum(jnp.where(fi == fj, diff_v[...].reshape(1, kinds), 0.0), axis=1, keepdims=True)
    fc = lax.broadcasted_iota(jnp.int32, (count, 1), 0)
    diff_col = diff_col + jnp.where((fc >= kinds) & (fc < kinds + own), 0.1, 0.0)
    react_pad[...] = jnp.zeros(react_pad.shape, F32)
    react_pad[0:kinds, 0:kinds] = react_v[...]
    mix = react_pad[...]
    mix_top = mix.astype(BF16).astype(F32)
    mix_rest = mix - mix_top
    mix_lhs = (mix_top + pltpu.roll(mix_top, kinds, 1) + pltpu.roll(mix_rest, 2 * kinds, 1)).astype(BF16)
    lane = lax.broadcasted_iota(jnp.int32, (count, width), 1)
    spare = jnp.zeros((128 - 3 * kinds, width), F32)

    def row_step(r, up, down):
        x = row_of(r)
        left = jnp.where(lane == 0, 0.0, pltpu.roll(x, 1, 1))
        right = jnp.where(lane == width - 1, 0.0, pltpu.roll(x, width - 1, 1))
        part = x[0:kinds]
        top = part.astype(BF16).astype(F32)
        rhs = jnp.concatenate([top, part - top, top, spare], axis=0).astype(BF16)
        mixed = jnp.dot(mix_lhs, rhs, preferred_element_type=F32)
        value = x + diff_col * (up + down + left + right - 4.0 * x) + mixed
        for b in range(blocks):
            flat_result[b, pl.ds(r, count, stride=rows), :] = value[:, b * 128:(b + 1) * 128]

    def inner(r, carry):
        row_step(r, row_of(r - 1), row_of(r + 1))
        return carry

    half = rows // 2
    lax.fori_loop(1, half, inner, 0)

    for step in range(1, nsec):
        got((me + step) % nsec, step).wait_recv()

    flat_dense = dense.reshape((sections + 2 * PAD) * 8, 128)
    flat_rate = rate.reshape(sections * 8, 128)
    acet = fields[me % blocks, 0, tile_rows(me), :]
    gap = jnp.zeros((128 - sections, 256), BF16)
    for pair in range(4):
        r0, r1 = 2 * pair, 2 * pair + 1

        def moved(t):
            start = 8 * (PAD - t)
            return jnp.concatenate(
                [flat_dense[pl.ds(start + r, sections, stride=8), :] for r in (r0, r1)], axis=1)

        held = moved(0)
        top, rest = split_bf16(held)
        rhs = jnp.concatenate([top, gap, rest, gap], axis=0)
        product = jnp.dot(lhs[:, 0:256], rhs, preferred_element_type=F32)
        product = product + jnp.dot(lhs[:, 256:384], rhs[0:128], preferred_element_type=F32)
        total = jnp.zeros((sections, 256), F32)
        for slot in range(SLOTS):
            total = total + moved(slot + LOW) * product[slot * sections:(slot + 1) * sections]
        growing = jnp.concatenate([acet[r0:r0 + 1], acet[r1:r1 + 1]], axis=1)
        flux = grow_col * held * growing
        total = total - flux + grow_prev * moved(1) * growing
        eaten = jnp.sum(flux, axis=0, keepdims=True)
        for n, r in enumerate((r0, r1)):
            flat_rate[pl.ds(r, sections, stride=8), :] = total[:, n * 128:(n + 1) * 128]
            used[r:r + 1, :] = eaten[:, n * 128:(n + 1) * 128]

    def rate_copy(p, source, step):
        return pltpu.make_async_remote_copy(
            src_ref=rate.at[pl.ds(own * p, own)], dst_ref=rate_in.at[source % blocks, :, tile_rows(source), :],
            send_sem=back_send.at[step], recv_sem=back_recv.at[source],
            device_id={"sec": p}, device_id_type=MESH)

    def used_copy(p, source, step):
        return pltpu.make_async_remote_copy(
            src_ref=used, dst_ref=used_in.at[source % blocks, tile_rows(source), :],
            send_sem=used_send.at[step], recv_sem=used_recv.at[source],
            device_id={"sec": p}, device_id_type=MESH)

    for step in range(1, nsec):
        p = (me + step) % nsec
        rate_copy(p, me, step).start()
        used_copy(p, me, step).start()
    rate_in[me % blocks, :, tile_rows(me), :] = rate[pl.ds(own * me, own)]
    used_in[me % blocks, tile_rows(me), :] = used[...]

    lax.fori_loop(half, rows - 1, inner, 0)
    edge(0).wait()
    edge(1).wait()
    row_step(0, jnp.where(at == 0, 0.0, edge_in[1]), row_of(1))
    row_step(rows - 1, row_of(rows - 2), jnp.where(at == nxs - 1, 0.0, edge_in[0]))

    for step in range(1, nsec):
        p = (me + step) % nsec
        rate_copy(p, p, step).wait_recv()
        used_copy(p, p, step).wait_recv()

    for step in range(1, nsec):
        p = (me + step) % nsec
        sent(p, step).wait_send()
        rate_copy(p, me, step).wait_send()
        used_copy(p, me, step).wait_send()


def finish(own, kinds, result, rate_in, used_in, stoich, soot_out, species_out, done, stoich_s, sem, small):
    blocks = result.shape[0]
    fetch = pltpu.make_async_copy(stoich, stoich_s, small)
    fetch.start()
    fetch.wait()
    stores = []
    for b in range(blocks):
        lanes = pl.ds(b * 128, 128)
        done[b, kinds:kinds + own] = result[b, kinds:kinds + own] + rate_in[b]
        used = used_in[b]
        for s in range(kinds):
            done[b, s] = result[b, s] - stoich_s[s] * used
        stores.append(pltpu.make_async_copy(done.at[b, pl.ds(0, kinds)], species_out.at[:, :, lanes], sem.at[b]))
        stores.append(pltpu.make_async_copy(done.at[b, pl.ds(kinds, own)], soot_out.at[:, :, lanes], sem.at[blocks + b]))
        stores[-2].start()
        stores[-1].start()
    for copy in stores:
        copy.wait()


def stay(x):
    return pltpu.with_memory_space_constraint(x, pltpu.HBM)


def shards(soot, species, kern, split, target, growth, diffusivity, reaction, stoich):
    own, rows, width = soot.shape
    kinds = species.shape[0]
    nsec, nxs = lax.axis_size("sec"), lax.axis_size("xs")
    sections = nsec * own
    blocks = width // 128
    count = -(-(kinds + own) // 8) * 8
    assert blocks * (rows // 8) == nsec and sections <= 128 and 3 * kinds <= 128
    dma = pltpu.SemaphoreType.DMA
    hbm = pl.BlockSpec(memory_space=pltpu.HBM)
    vmem = pl.BlockSpec(memory_space=pltpu.VMEM)
    parts = pl.pallas_call(
        functools.partial(kernel, nsec, nxs, own, kinds),
        out_shape=(
            jax.ShapeDtypeStruct((blocks, count, rows, 128), F32),
            jax.ShapeDtypeStruct((blocks, own, rows, 128), F32),
            jax.ShapeDtypeStruct((blocks, rows, 128), F32),
        ),
        in_specs=[hbm] * 8,
        out_specs=(vmem, vmem, vmem),
        scratch_shapes=[
            pltpu.VMEM((blocks, count, rows, 128), F32),
            pltpu.VMEM((sections + 2 * PAD, 8, 128), F32),
            pltpu.VMEM((sections, 8, 128), F32),
            pltpu.VMEM((8, 128), F32),
            pltpu.VMEM((2, count, width), F32),
            pltpu.VMEM((2, count, width), F32),
            pltpu.VMEM(kern.shape, F32),
            pltpu.VMEM(split.shape, F32),
            pltpu.VMEM(target.shape, jnp.int32),
            pltpu.VMEM(growth.shape, F32),
            pltpu.VMEM(diffusivity.shape, F32),
            pltpu.VMEM(reaction.shape, F32),
            pltpu.VMEM((count, 128), F32),
            pltpu.VMEM((SLOTS, sections + 2 * PAD, 128), F32),
            pltpu.VMEM((SLOTS * sections, 384), BF16),
            dma((1 + 2 * blocks + 6,)),
            dma((nsec,)), dma((nsec,)), dma((nsec,)), dma((nsec,)), dma((nsec,)), dma((nsec,)),
            dma((2,)), dma((2,)),
        ],
        compiler_params=pltpu.CompilerParams(
            collective_id=0, has_side_effects=True, vmem_limit_bytes=32 << 20),
    )(*(stay(x) for x in (soot, species, kern, split, target, growth, diffusivity, reaction)))
    return pl.pallas_call(
        functools.partial(finish, own, kinds),
        out_shape=(jax.ShapeDtypeStruct(soot.shape, F32), jax.ShapeDtypeStruct(species.shape, F32)),
        in_specs=[vmem, vmem, vmem, hbm],
        out_specs=(hbm, hbm),
        scratch_shapes=[
            pltpu.VMEM((blocks, count, rows, 128), F32),
            pltpu.SMEM(stoich.shape, F32),
            dma((2 * blocks,)),
            dma(()),
        ],
        compiler_params=pltpu.CompilerParams(vmem_limit_bytes=16 << 20),
    )(*parts, stay(stoich))


def solution(mesh):
    return jax.shard_map(
        shards,
        mesh=mesh,
        in_specs=(P("sec", "xs", None), P(None, "xs", None), P(), P(), P(), P(), P(), P(), P()),
        out_specs=(P("sec", "xs", None), P(None, "xs", None)),
        check_vma=False,
    )
```

```python
import functools

import jax
import jax.numpy as jnp
from jax import lax
from jax.experimental import pallas as pl
from jax.experimental.pallas import tpu as pltpu
from jax.sharding import PartitionSpec as P

MESH = pl.DeviceIdType.MESH
F32, BF16 = jnp.float32, jnp.bfloat16
PAD = 8
PART = 4
PARTS = 8 // PART
ROWS_BEFORE = (5, 10)
ORDER = (3, 13, 11, 5, 4, 12, 2, 14, 10, 6, 1, 15, 9, 7, 8)
LOW, HIGH = -1, 4
SLOTS = HIGH - LOW + 1


def split_bf16(x):
    high = x.astype(BF16)
    return high, (x - high.astype(F32)).astype(BF16)


def kernel(
    nsec, nxs, own, kinds,
    soot, species, kern, split, target, growth, diffusivity, reaction, stoich,
    result,
    fields, dense, rate, used, rate_in, used_in,
    edge_out, edge_in, kern_v, split_v, target_v, growth_v, diff_v, react_v, stoich_s,
    react_pad, weights, lhs,
    load_sem, send_sem, recv_sem, back_send, back_recv, used_send, used_recv, edge_send, edge_recv, ready,
):
    sections = nsec * own
    count = fields.shape[1]
    rows = fields.shape[2]
    blocks = fields.shape[0]
    width = blocks * 128
    me = lax.axis_index("sec")
    at = lax.axis_index("xs")
    before, after = (at + nxs - 1) % nxs, (at + 1) % nxs

    barrier = pltpu.get_barrier_semaphore()
    for step in range(1, nsec):
        pl.semaphore_signal(barrier, inc=1, device_id={"sec": (me + step) % nsec}, device_id_type=MESH)

    @pl.when(at < nxs - 1)
    def _():
        pl.semaphore_signal(barrier, inc=1, device_id={"xs": after}, device_id_type=MESH)


    def tile_rows(p):
        return pl.ds(pl.multiple_of((p // blocks) * 8, 8), 8)

    def part_rows(p, part):
        return pl.ds(pl.multiple_of((p // blocks) * 8 + part * PART, PART), PART)

    def lanes_of(p):
        return pl.ds(pl.multiple_of((p % blocks) * 128, 128), 128)

    loads = [pltpu.make_async_copy(soot.at[:, tile_rows(me), lanes_of(me)], dense.at[pl.ds(PAD + own * me, own)], load_sem.at[0])]
    for b in range(blocks):
        lanes = pl.ds(b * 128, 128)
        loads.append(pltpu.make_async_copy(species.at[:, :, lanes], fields.at[b, pl.ds(0, kinds)], load_sem.at[1 + b]))
        loads.append(pltpu.make_async_copy(soot.at[:, :, lanes], fields.at[b, pl.ds(kinds, own)], load_sem.at[1 + blocks + b]))
    tables = [(kern, kern_v), (split, split_v), (target, target_v), (growth, growth_v), (diffusivity, diff_v), (reaction, react_v), (stoich, stoich_s)]
    for n, (src, dst) in enumerate(tables):
        loads.append(pltpu.make_async_copy(src, dst, load_sem.at[1 + 2 * blocks + n]))
    for copy in loads:
        copy.start()

    @pl.when(at == 0)
    def _():
        pl.semaphore_wait(barrier, nsec - 1)

    @pl.when(at > 0)
    def _():
        pl.semaphore_wait(barrier, nsec)
        pl.semaphore_signal(ready, inc=1, device_id={"xs": before}, device_id_type=MESH)

    def cells(p, source, step, part):
        return pltpu.make_async_remote_copy(
            src_ref=soot.at[:, part_rows(p, part), lanes_of(p)],
            dst_ref=dense.at[pl.ds(PAD + own * source, own), pl.ds(part * PART, PART)],
            send_sem=send_sem.at[part, step], recv_sem=recv_sem.at[part, source],
            device_id={"sec": p}, device_id_type=MESH)

    for part in range(PARTS):
        for step in ORDER:
            cells((me + step) % nsec, me, step, part).start()

    zero_tiles = jnp.zeros((PAD, 8, 128), F32)
    dense[0:PAD] = zero_tiles
    dense[PAD + sections:] = zero_tiles
    fields[:, kinds + own:] = jnp.zeros((blocks, count - kinds - own, rows, 128), F32)
    for copy in loads:
        copy.wait()

    flat = fields.reshape(blocks, count * rows, 128)
    flat_result = result.reshape(blocks, count * rows, 128)

    def row_of(r):
        return jnp.concatenate([flat[b, pl.ds(r, count, stride=rows), :] for b in range(blocks)], axis=1)

    edge_out[0] = row_of(0)
    edge_out[1] = row_of(rows - 1)

    def edge(side):
        return pltpu.make_async_remote_copy(
            src_ref=edge_out.at[side], dst_ref=edge_in.at[side],
            send_sem=edge_send.at[side], recv_sem=edge_recv.at[side],
            device_id={"xs": before if side == 0 else after}, device_id_type=MESH)

    @pl.when(at > 0)
    def _():
        edge(0).start()

    @pl.when(at == 0)
    def _():
        edge_in[1] = jnp.zeros((count, width), F32)

    @pl.when(at == nxs - 1)
    def _():
        edge_in[0] = jnp.zeros((count, width), F32)

    i = lax.broadcasted_iota(jnp.int32, (sections, sections), 0)
    j = lax.broadcasted_iota(jnp.int32, (sections, sections), 1)
    rates = kern_v[...]
    shares = split_v[...]
    goal = target_v[...]
    low = 0.5 * rates * shares
    high = 0.5 * rates * (1.0 - shares)
    low_t, high_t, goal_t = low.T, high.T, goal.T
    weights[...] = jnp.zeros(weights.shape, F32)
    for slot in range(SLOTS):
        t = slot + LOW
        lower = jnp.where(goal == i + t, low, 0.0) + jnp.where(goal == i + (t - 1), high, 0.0)
        upper = jnp.where(goal_t == i + t, low_t, 0.0) + jnp.where(goal_t == i + (t - 1), high_t, 0.0)
        value = jnp.where(j <= i, lower, 0.0) + jnp.where(j < i, upper, 0.0)
        if t == 0:
            value = value - rates
        weights[slot, PAD + t:PAD + t + sections, 0:sections] = value
    for slot in range(SLOTS):
        top, rest = split_bf16(weights[slot, PAD:PAD + sections, :])
        here = pl.ds(slot * sections, sections)
        lhs[here, 0:128] = top
        lhs[here, 128:256] = top
        lhs[here, 256:384] = rest
    grow = growth_v[...].reshape(1, sections)
    grow_col = jnp.sum(jnp.where(i == j, grow, 0.0), axis=1, keepdims=True)
    grow_prev = jnp.sum(jnp.where(i == j + 1, grow, 0.0), axis=1, keepdims=True)

    fi = lax.broadcasted_iota(jnp.int32, (count, kinds), 0)
    fj = lax.broadcasted_iota(jnp.int32, (count, kinds), 1)
    diff_col = jnp.sum(jnp.where(fi == fj, diff_v[...].reshape(1, kinds), 0.0), axis=1, keepdims=True)
    fc = lax.broadcasted_iota(jnp.int32, (count, 1), 0)
    diff_col = diff_col + jnp.where((fc >= kinds) & (fc < kinds + own), 0.1, 0.0)
    react_pad[...] = jnp.zeros(react_pad.shape, F32)
    react_pad[0:kinds, 0:kinds] = react_v[...]
    mix = react_pad[...]
    mix_top = mix.astype(BF16).astype(F32)
    mix_rest = mix - mix_top
    mix_lhs = (mix_top + pltpu.roll(mix_top, kinds, 1) + pltpu.roll(mix_rest, 2 * kinds, 1)).astype(BF16)
    lane = lax.broadcasted_iota(jnp.int32, (count, width), 1)
    spare = jnp.zeros((128 - 3 * kinds, width), F32)

    def row_step(r, up, down):
        x = row_of(r)
        left = jnp.where(lane == 0, 0.0, pltpu.roll(x, 1, 1))
        right = jnp.where(lane == width - 1, 0.0, pltpu.roll(x, width - 1, 1))
        part = x[0:kinds]
        top = part.astype(BF16).astype(F32)
        rhs = jnp.concatenate([top, part - top, top, spare], axis=0).astype(BF16)
        mixed = jnp.dot(mix_lhs, rhs, preferred_element_type=F32)
        value = x + diff_col * (up + down + left + right - 4.0 * x) + mixed
        for b in range(blocks):
            flat_result[b, pl.ds(r, count, stride=rows), :] = value[:, b * 128:(b + 1) * 128]

    def inner(r, carry):
        row_step(r, row_of(r - 1), row_of(r + 1))
        return carry

    flat_dense = dense.reshape((sections + 2 * PAD) * 8, 128)
    flat_rate = rate.reshape(sections * 8, 128)
    acet = fields[me % blocks, 0, tile_rows(me), :]
    gap = jnp.zeros((128 - sections, 256), BF16)

    def rate_pair(pair):
        r0, r1 = 2 * pair, 2 * pair + 1

        def moved(t):
            start = 8 * (PAD - t)
            return jnp.concatenate(
                [flat_dense[pl.ds(start + r, sections, stride=8), :] for r in (r0, r1)], axis=1)

        held = moved(0)
        top, rest = split_bf16(held)
        rhs = jnp.concatenate([top, gap, rest, gap], axis=0)
        product = jnp.dot(lhs[:, 0:256], rhs, preferred_element_type=F32)
        product = product + jnp.dot(lhs[:, 256:384], rhs[0:128], preferred_element_type=F32)
        total = jnp.zeros((sections, 256), F32)
        for slot in range(SLOTS):
            total = total + moved(slot + LOW) * product[slot * sections:(slot + 1) * sections]
        growing = jnp.concatenate([acet[r0:r0 + 1], acet[r1:r1 + 1]], axis=1)
        flux = grow_col * held * growing
        total = total - flux + grow_prev * moved(1) * growing
        eaten = jnp.sum(flux, axis=0, keepdims=True)
        for n, r in enumerate((r0, r1)):
            flat_rate[pl.ds(r, sections, stride=8), :] = total[:, n * 128:(n + 1) * 128]
            used[r:r + 1, :] = eaten[:, n * 128:(n + 1) * 128]

    def rate_copy(p, source, step, part):
        return pltpu.make_async_remote_copy(
            src_ref=rate.at[pl.ds(own * p, own), pl.ds(part * PART, PART)],
            dst_ref=rate_in.at[source % blocks, :, part_rows(source, part), :],
            send_sem=back_send.at[part, step], recv_sem=back_recv.at[part, source],
            device_id={"sec": p}, device_id_type=MESH)

    def used_copy(p, source, step, part):
        return pltpu.make_async_remote_copy(
            src_ref=used.at[pl.ds(part * PART, PART)],
            dst_ref=used_in.at[source % blocks, part_rows(source, part), :],
            send_sem=used_send.at[part, step], recv_sem=used_recv.at[part, source],
            device_id={"sec": p}, device_id_type=MESH)

    first = 1
    for part in range(PARTS):
        last = ROWS_BEFORE[part]
        lax.fori_loop(first, last, inner, 0)
        first = last
        for step in range(1, nsec):
            p = (me + step) % nsec
            cells(p, p, step, part).wait_recv()
        for pair in range(part * PART // 2, (part + 1) * PART // 2):
            rate_pair(pair)
        for step in ORDER:
            used_copy((me + step) % nsec, me, step, part).start()
        for step in ORDER:
            rate_copy((me + step) % nsec, me, step, part).start()
        if part == 0:
            @pl.when(at < nxs - 1)
            def _():
                pl.semaphore_wait(ready, 1)
                edge(1).start()
    rate_in[me % blocks, :, tile_rows(me), :] = rate[pl.ds(own * me, own)]
    used_in[me % blocks, tile_rows(me), :] = used[...]

    lax.fori_loop(first, rows - 1, inner, 0)

    @pl.when(at > 0)
    def _():
        edge(0).wait_send()
        edge(1).wait_recv()

    @pl.when(at < nxs - 1)
    def _():
        edge(1).wait_send()
        edge(0).wait_recv()

    row_step(0, edge_in[1], row_of(1))
    row_step(rows - 1, row_of(rows - 2), edge_in[0])

    for part in range(PARTS):
        for step in range(1, nsec):
            p = (me + step) % nsec
            used_copy(p, p, step, part).wait_recv()

    def consume(s, carry):
        result[:, s] = result[:, s] - stoich_s[s] * used_in[...]
        return carry

    lax.fori_loop(0, kinds, consume, 0)
    for part in range(PARTS):
        for step in range(1, nsec):
            p = (me + step) % nsec
            rate_copy(p, p, step, part).wait_recv()
    result[:, kinds:kinds + own] = result[:, kinds:kinds + own] + rate_in[...]
    for part in range(PARTS):
        for step in range(1, nsec):
            p = (me + step) % nsec
            cells(p, me, step, part).wait_send()
            rate_copy(p, me, step, part).wait_send()
            used_copy(p, me, step, part).wait_send()


def write_out(own, kinds, result, soot_out, species_out, sem):
    blocks = result.shape[0]
    stores = []
    for b in range(blocks):
        lanes = pl.ds(b * 128, 128)
        stores.append(pltpu.make_async_copy(result.at[b, pl.ds(0, kinds)], species_out.at[:, :, lanes], sem.at[b]))
        stores.append(pltpu.make_async_copy(result.at[b, pl.ds(kinds, own)], soot_out.at[:, :, lanes], sem.at[blocks + b]))
    for copy in stores:
        copy.start()
    for copy in stores:
        copy.wait()


def stay(x):
    return pltpu.with_memory_space_constraint(x, pltpu.HBM)


def shards(soot, species, kern, split, target, growth, diffusivity, reaction, stoich):
    own, rows, width = soot.shape
    kinds = species.shape[0]
    nsec, nxs = lax.axis_size("sec"), lax.axis_size("xs")
    sections = nsec * own
    blocks = width // 128
    count = -(-(kinds + own) // 8) * 8
    assert blocks * (rows // 8) == nsec and sections <= 128 and 3 * kinds <= 128
    dma = pltpu.SemaphoreType.DMA
    hbm = pl.BlockSpec(memory_space=pltpu.HBM)
    vmem = pl.BlockSpec(memory_space=pltpu.VMEM)
    parts = pl.pallas_call(
        functools.partial(kernel, nsec, nxs, own, kinds),
        out_shape=jax.ShapeDtypeStruct((blocks, count, rows, 128), F32),
        in_specs=[hbm] * 9,
        out_specs=vmem,
        scratch_shapes=[
            pltpu.VMEM((blocks, count, rows, 128), F32),
            pltpu.VMEM((sections + 2 * PAD, 8, 128), F32),
            pltpu.VMEM((sections, 8, 128), F32),
            pltpu.VMEM((8, 128), F32),
            pltpu.VMEM((blocks, own, rows, 128), F32),
            pltpu.VMEM((blocks, rows, 128), F32),
            pltpu.VMEM((2, count, width), F32),
            pltpu.VMEM((2, count, width), F32),
            pltpu.VMEM(kern.shape, F32),
            pltpu.VMEM(split.shape, F32),
            pltpu.VMEM(target.shape, jnp.int32),
            pltpu.VMEM(growth.shape, F32),
            pltpu.VMEM(diffusivity.shape, F32),
            pltpu.VMEM(reaction.shape, F32),
            pltpu.SMEM(stoich.shape, F32),
            pltpu.VMEM((count, 128), F32),
            pltpu.VMEM((SLOTS, sections + 2 * PAD, 128), F32),
            pltpu.VMEM((SLOTS * sections, 384), BF16),
            dma((1 + 2 * blocks + 7,)),
            *[dma((PARTS, nsec))] * 6,
            dma((2,)), dma((2,)), pltpu.SemaphoreType.REGULAR,
        ],
        compiler_params=pltpu.CompilerParams(
            collective_id=0, has_side_effects=True, vmem_limit_bytes=32 << 20),
    )(*(stay(x) for x in (soot, species, kern, split, target, growth, diffusivity, reaction, stoich)))
    return pl.pallas_call(
        functools.partial(write_out, own, kinds),
        out_shape=(jax.ShapeDtypeStruct(soot.shape, F32), jax.ShapeDtypeStruct(species.shape, F32)),
        in_specs=[vmem],
        out_specs=(hbm, hbm),
        scratch_shapes=[dma((2 * blocks,))],
        compiler_params=pltpu.CompilerParams(vmem_limit_bytes=4 << 20),
    )(parts)


def solution(mesh):
    return jax.shard_map(
        shards,
        mesh=mesh,
        in_specs=(P("sec", "xs", None), P(None, "xs", None), P(), P(), P(), P(), P(), P(), P()),
        out_specs=(P("sec", "xs", None), P(None, "xs", None)),
        check_vma=False,
    )
```

```python
import functools

import jax
import jax.numpy as jnp
from jax import lax
from jax.experimental import pallas as pl
from jax.experimental.pallas import tpu as pltpu
from jax.sharding import PartitionSpec as P

MESH = pl.DeviceIdType.MESH
F32, BF16 = jnp.float32, jnp.bfloat16
PAD = 8
PART = 4
PARTS = 8 // PART
ROWS_BEFORE = (5, 10)
USED_ORDER = (4, 3, 5, 2, 6, 1, 7)
ORDER = (3, 13, 11, 5, 4, 12, 2, 14, 10, 6, 1, 15, 9, 7, 8)
LOW, HIGH = -1, 4
SLOTS = HIGH - LOW + 1


def split_bf16(x):
    high = x.astype(BF16)
    return high, (x - high.astype(F32)).astype(BF16)


def kernel(
    nsec, nxs, own, kinds,
    soot, species, kern, split, target, growth, diffusivity, reaction, stoich,
    result,
    fields, dense, rate, used, rate_in, used_in,
    edge_out, edge_in, kern_v, split_v, target_v, growth_v, diff_v, react_v, stoich_s,
    react_pad, weights, lhs,
    load_sem, send_sem, recv_sem, back_send, back_recv, used_send, used_recv, edge_send, edge_recv, ready,
):
    sections = nsec * own
    count = fields.shape[1]
    rows = fields.shape[2]
    blocks = fields.shape[0]
    width = blocks * 128
    me = lax.axis_index("sec")
    at = lax.axis_index("xs")
    before, after = (at + nxs - 1) % nxs, (at + 1) % nxs

    barrier = pltpu.get_barrier_semaphore()
    for step in range(1, nsec):
        pl.semaphore_signal(barrier, inc=1, device_id={"sec": (me + step) % nsec}, device_id_type=MESH)

    @pl.when(at < nxs - 1)
    def _():
        pl.semaphore_signal(barrier, inc=1, device_id={"xs": after}, device_id_type=MESH)


    def tile_rows(p):
        return pl.ds(pl.multiple_of((p // blocks) * 8, 8), 8)

    def part_rows(p, part):
        return pl.ds(pl.multiple_of((p // blocks) * 8 + part * PART, PART), PART)

    def lanes_of(p):
        return pl.ds(pl.multiple_of((p % blocks) * 128, 128), 128)

    loads = [pltpu.make_async_copy(soot.at[:, tile_rows(me), lanes_of(me)], dense.at[pl.ds(PAD + own * me, own)], load_sem.at[0])]
    for b in range(blocks):
        lanes = pl.ds(b * 128, 128)
        loads.append(pltpu.make_async_copy(species.at[:, :, lanes], fields.at[b, pl.ds(0, kinds)], load_sem.at[1 + b]))
        loads.append(pltpu.make_async_copy(soot.at[:, :, lanes], fields.at[b, pl.ds(kinds, own)], load_sem.at[1 + blocks + b]))
    tables = [(kern, kern_v), (split, split_v), (target, target_v), (growth, growth_v), (diffusivity, diff_v), (reaction, react_v), (stoich, stoich_s)]
    for n, (src, dst) in enumerate(tables):
        loads.append(pltpu.make_async_copy(src, dst, load_sem.at[1 + 2 * blocks + n]))
    for copy in loads:
        copy.start()

    @pl.when(at == 0)
    def _():
        pl.semaphore_wait(barrier, nsec - 1)

    @pl.when(at > 0)
    def _():
        pl.semaphore_wait(barrier, nsec)
        pl.semaphore_signal(ready, inc=1, device_id={"xs": before}, device_id_type=MESH)

    def cells(p, source, part):
        return pltpu.make_async_remote_copy(
            src_ref=soot.at[:, part_rows(p, part), lanes_of(p)],
            dst_ref=dense.at[pl.ds(PAD + own * source, own), pl.ds(part * PART, PART)],
            send_sem=send_sem.at[part], recv_sem=recv_sem.at[part],
            device_id={"sec": p}, device_id_type=MESH)

    peers = pl.ds(PAD, own * (nsec - 1))

    def all_cells(part):
        piece = dense.at[peers, pl.ds(part * PART, PART)]
        return pltpu.make_async_remote_copy(
            src_ref=piece, dst_ref=piece, send_sem=send_sem.at[part], recv_sem=recv_sem.at[part],
            device_id={"sec": (me + 1) % nsec}, device_id_type=MESH)

    for part in range(PARTS):
        for step in ORDER:
            cells((me + step) % nsec, me, part).start()

    zero_tiles = jnp.zeros((PAD, 8, 128), F32)
    dense[0:PAD] = zero_tiles
    dense[PAD + sections:] = zero_tiles
    fields[:, kinds + own:] = jnp.zeros((blocks, count - kinds - own, rows, 128), F32)
    for copy in loads:
        copy.wait()

    flat = fields.reshape(blocks, count * rows, 128)
    flat_result = result.reshape(blocks, count * rows, 128)

    def row_of(r):
        return jnp.concatenate([flat[b, pl.ds(r, count, stride=rows), :] for b in range(blocks)], axis=1)

    edge_out[0] = row_of(0)
    edge_out[1] = row_of(rows - 1)

    def edge(side):
        return pltpu.make_async_remote_copy(
            src_ref=edge_out.at[side], dst_ref=edge_in.at[side],
            send_sem=edge_send.at[side], recv_sem=edge_recv.at[side],
            device_id={"xs": before if side == 0 else after}, device_id_type=MESH)

    @pl.when(at > 0)
    def _():
        edge(0).start()

    @pl.when(at == 0)
    def _():
        edge_in[1] = jnp.zeros((count, width), F32)

    @pl.when(at == nxs - 1)
    def _():
        edge_in[0] = jnp.zeros((count, width), F32)

    i = lax.broadcasted_iota(jnp.int32, (sections, sections), 0)
    j = lax.broadcasted_iota(jnp.int32, (sections, sections), 1)
    rates = kern_v[...]
    shares = split_v[...]
    goal = target_v[...]
    low = 0.5 * rates * shares
    high = 0.5 * rates * (1.0 - shares)
    low_t, high_t, goal_t = low.T, high.T, goal.T
    weights[...] = jnp.zeros(weights.shape, F32)
    for slot in range(SLOTS):
        t = slot + LOW
        lower = jnp.where(goal == i + t, low, 0.0) + jnp.where(goal == i + (t - 1), high, 0.0)
        upper = jnp.where(goal_t == i + t, low_t, 0.0) + jnp.where(goal_t == i + (t - 1), high_t, 0.0)
        value = jnp.where(j <= i, lower, 0.0) + jnp.where(j < i, upper, 0.0)
        if t == 0:
            value = value - rates
        weights[slot, PAD + t:PAD + t + sections, 0:sections] = value
    for slot in range(SLOTS):
        top, rest = split_bf16(weights[slot, PAD:PAD + sections, :])
        here = pl.ds(slot * sections, sections)
        lhs[here, 0:128] = top
        lhs[here, 128:256] = top
        lhs[here, 256:384] = rest
    grow = growth_v[...].reshape(1, sections)
    grow_col = jnp.sum(jnp.where(i == j, grow, 0.0), axis=1, keepdims=True)
    grow_prev = jnp.sum(jnp.where(i == j + 1, grow, 0.0), axis=1, keepdims=True)

    fi = lax.broadcasted_iota(jnp.int32, (count, kinds), 0)
    fj = lax.broadcasted_iota(jnp.int32, (count, kinds), 1)
    diff_col = jnp.sum(jnp.where(fi == fj, diff_v[...].reshape(1, kinds), 0.0), axis=1, keepdims=True)
    fc = lax.broadcasted_iota(jnp.int32, (count, 1), 0)
    diff_col = diff_col + jnp.where((fc >= kinds) & (fc < kinds + own), 0.1, 0.0)
    react_pad[...] = jnp.zeros(react_pad.shape, F32)
    react_pad[0:kinds, 0:kinds] = react_v[...]
    mix = react_pad[...]
    mix_top = mix.astype(BF16).astype(F32)
    mix_rest = mix - mix_top
    mix_lhs = (mix_top + pltpu.roll(mix_top, kinds, 1) + pltpu.roll(mix_rest, 2 * kinds, 1)).astype(BF16)
    lane = lax.broadcasted_iota(jnp.int32, (count, width), 1)
    spare = jnp.zeros((128 - 3 * kinds, width), F32)

    def row_step(r, up, down):
        x = row_of(r)
        left = jnp.where(lane == 0, 0.0, pltpu.roll(x, 1, 1))
        right = jnp.where(lane == width - 1, 0.0, pltpu.roll(x, width - 1, 1))
        part = x[0:kinds]
        top = part.astype(BF16).astype(F32)
        rhs = jnp.concatenate([top, part - top, top, spare], axis=0).astype(BF16)
        mixed = jnp.dot(mix_lhs, rhs, preferred_element_type=F32)
        value = x + diff_col * (up + down + left + right - 4.0 * x) + mixed
        for b in range(blocks):
            flat_result[b, pl.ds(r, count, stride=rows), :] = value[:, b * 128:(b + 1) * 128]

    def inner(r, carry):
        row_step(r, row_of(r - 1), row_of(r + 1))
        return carry

    flat_dense = dense.reshape((sections + 2 * PAD) * 8, 128)
    flat_rate = rate.reshape(sections * 8, 128)
    acet = fields[me % blocks, 0, tile_rows(me), :]
    gap = jnp.zeros((128 - sections, 256), BF16)

    def rate_pair(pair):
        r0, r1 = 2 * pair, 2 * pair + 1

        def moved(t):
            start = 8 * (PAD - t)
            return jnp.concatenate(
                [flat_dense[pl.ds(start + r, sections, stride=8), :] for r in (r0, r1)], axis=1)

        held = moved(0)
        top, rest = split_bf16(held)
        rhs = jnp.concatenate([top, gap, rest, gap], axis=0)
        product = jnp.dot(lhs[:, 0:256], rhs, preferred_element_type=F32)
        product = product + jnp.dot(lhs[:, 256:384], rhs[0:128], preferred_element_type=F32)
        total = jnp.zeros((sections, 256), F32)
        for slot in range(SLOTS):
            total = total + moved(slot + LOW) * product[slot * sections:(slot + 1) * sections]
        growing = jnp.concatenate([acet[r0:r0 + 1], acet[r1:r1 + 1]], axis=1)
        flux = grow_col * held * growing
        total = total - flux + grow_prev * moved(1) * growing
        eaten = jnp.sum(flux, axis=0, keepdims=True)
        for n, r in enumerate((r0, r1)):
            flat_rate[pl.ds(r, sections, stride=8), :] = total[:, n * 128:(n + 1) * 128]
            used[r:r + 1, :] = eaten[:, n * 128:(n + 1) * 128]

    def rate_copy(p, source, part):
        return pltpu.make_async_remote_copy(
            src_ref=rate.at[pl.ds(own * p, own), pl.ds(part * PART, PART)],
            dst_ref=rate_in.at[source % blocks, :, part_rows(source, part), :],
            send_sem=back_send.at[part], recv_sem=back_recv.at[part],
            device_id={"sec": p}, device_id_type=MESH)

    def all_rates(part):
        piece = rate.at[pl.ds(0, own * (nsec - 1)), pl.ds(part * PART, PART)]
        return pltpu.make_async_remote_copy(
            src_ref=piece, dst_ref=piece, send_sem=back_send.at[part], recv_sem=back_recv.at[part],
            device_id={"sec": (me + 1) % nsec}, device_id_type=MESH)

    plane, place = me // blocks, me % blocks
    planes = nsec // blocks

    def used_copy(step):
        return pltpu.make_async_remote_copy(
            src_ref=used, dst_ref=used_in.at[place, tile_rows(me), :],
            send_sem=used_send.at[0], recv_sem=used_recv.at[0],
            device_id={"sec": plane * blocks + (place + step) % blocks}, device_id_type=MESH)

    def all_used():
        piece = used_in.at[pl.ds(0, blocks - 1), pl.ds(0, 8), :]
        return pltpu.make_async_remote_copy(
            src_ref=piece, dst_ref=piece, send_sem=used_send.at[0], recv_sem=used_recv.at[0],
            device_id={"sec": plane * blocks + (place + 1) % blocks}, device_id_type=MESH)

    def pass_on(step, source):
        piece = used_in.at[:, pl.ds(pl.multiple_of(source * 8, 8), 8), :]
        return pltpu.make_async_remote_copy(
            src_ref=piece, dst_ref=piece,
            send_sem=used_send.at[step], recv_sem=used_recv.at[step],
            device_id={"sec": (plane + step) % planes * blocks + place}, device_id_type=MESH)

    first = 1
    for part in range(PARTS):
        last = ROWS_BEFORE[part]
        lax.fori_loop(first, last, inner, 0)
        first = last
        all_cells(part).wait_recv()
        for pair in range(part * PART // 2, (part + 1) * PART // 2):
            rate_pair(pair)
        if part == PARTS - 1:
            used_in[place, tile_rows(me), :] = used[...]
            for step in USED_ORDER:
                used_copy(step).start()
        for step in ORDER:
            rate_copy((me + step) % nsec, me, part).start()
        if part == 0:
            @pl.when(at < nxs - 1)
            def _():
                pl.semaphore_wait(ready, 1)
                edge(1).start()
    rate_in[me % blocks, :, tile_rows(me), :] = rate[pl.ds(own * me, own)]

    lax.fori_loop(first, rows - 1, inner, 0)

    @pl.when(at > 0)
    def _():
        edge(0).wait_send()
        edge(1).wait_recv()

    @pl.when(at < nxs - 1)
    def _():
        edge(1).wait_send()
        edge(0).wait_recv()

    row_step(0, edge_in[1], row_of(1))
    row_step(rows - 1, row_of(rows - 2), edge_in[0])

    all_used().wait_recv()
    for step in range(1, planes):
        pass_on(step, plane).start()
    for step in range(1, planes):
        pass_on(step, (plane - step + planes) % planes).wait_recv()

    def consume(s, carry):
        result[:, s] = result[:, s] - stoich_s[s] * used_in[...]
        return carry

    lax.fori_loop(0, kinds, consume, 0)
    for part in range(PARTS):
        all_rates(part).wait_recv()
    result[:, kinds:kinds + own] = result[:, kinds:kinds + own] + rate_in[...]
    for part in range(PARTS):
        all_cells(part).wait_send()
        all_rates(part).wait_send()
    all_used().wait_send()
    for step in range(1, planes):
        pass_on(step, plane).wait_send()


def write_out(own, kinds, result, soot_out, species_out, sem):
    blocks = result.shape[0]
    stores = []
    for b in range(blocks):
        lanes = pl.ds(b * 128, 128)
        stores.append(pltpu.make_async_copy(result.at[b, pl.ds(0, kinds)], species_out.at[:, :, lanes], sem.at[b]))
        stores.append(pltpu.make_async_copy(result.at[b, pl.ds(kinds, own)], soot_out.at[:, :, lanes], sem.at[blocks + b]))
    for copy in stores:
        copy.start()
    for copy in stores:
        copy.wait()


def stay(x):
    return pltpu.with_memory_space_constraint(x, pltpu.HBM)


def shards(soot, species, kern, split, target, growth, diffusivity, reaction, stoich):
    own, rows, width = soot.shape
    kinds = species.shape[0]
    nsec, nxs = lax.axis_size("sec"), lax.axis_size("xs")
    sections = nsec * own
    blocks = width // 128
    count = -(-(kinds + own) // 8) * 8
    assert blocks * (rows // 8) == nsec and sections <= 128 and 3 * kinds <= 128
    dma = pltpu.SemaphoreType.DMA
    hbm = pl.BlockSpec(memory_space=pltpu.HBM)
    vmem = pl.BlockSpec(memory_space=pltpu.VMEM)
    parts = pl.pallas_call(
        functools.partial(kernel, nsec, nxs, own, kinds),
        out_shape=jax.ShapeDtypeStruct((blocks, count, rows, 128), F32),
        in_specs=[hbm] * 9,
        out_specs=vmem,
        scratch_shapes=[
            pltpu.VMEM((blocks, count, rows, 128), F32),
            pltpu.VMEM((sections + 2 * PAD, 8, 128), F32),
            pltpu.VMEM((sections, 8, 128), F32),
            pltpu.VMEM((8, 128), F32),
            pltpu.VMEM((blocks, own, rows, 128), F32),
            pltpu.VMEM((blocks, rows, 128), F32),
            pltpu.VMEM((2, count, width), F32),
            pltpu.VMEM((2, count, width), F32),
            pltpu.VMEM(kern.shape, F32),
            pltpu.VMEM(split.shape, F32),
            pltpu.VMEM(target.shape, jnp.int32),
            pltpu.VMEM(growth.shape, F32),
            pltpu.VMEM(diffusivity.shape, F32),
            pltpu.VMEM(reaction.shape, F32),
            pltpu.SMEM(stoich.shape, F32),
            pltpu.VMEM((count, 128), F32),
            pltpu.VMEM((SLOTS, sections + 2 * PAD, 128), F32),
            pltpu.VMEM((SLOTS * sections, 384), BF16),
            dma((1 + 2 * blocks + 7,)),
            *[dma((PARTS,))] * 4, *[dma((nsec // blocks,))] * 2,
            dma((2,)), dma((2,)), pltpu.SemaphoreType.REGULAR,
        ],
        compiler_params=pltpu.CompilerParams(
            collective_id=0, has_side_effects=True, vmem_limit_bytes=32 << 20),
    )(*(stay(x) for x in (soot, species, kern, split, target, growth, diffusivity, reaction, stoich)))
    return pl.pallas_call(
        functools.partial(write_out, own, kinds),
        out_shape=(jax.ShapeDtypeStruct(soot.shape, F32), jax.ShapeDtypeStruct(species.shape, F32)),
        in_specs=[vmem],
        out_specs=(hbm, hbm),
        scratch_shapes=[dma((2 * blocks,))],
        compiler_params=pltpu.CompilerParams(vmem_limit_bytes=4 << 20),
    )(parts)


def solution(mesh):
    return jax.shard_map(
        shards,
        mesh=mesh,
        in_specs=(P("sec", "xs", None), P(None, "xs", None), P(), P(), P(), P(), P(), P(), P()),
        out_specs=(P("sec", "xs", None), P(None, "xs", None)),
        check_vma=False,
    )
```

```python
import functools

import jax
import jax.numpy as jnp
from jax import lax
from jax.experimental import pallas as pl
from jax.experimental.pallas import tpu as pltpu
from jax.sharding import PartitionSpec as P

MESH = pl.DeviceIdType.MESH
F32, BF16 = jnp.float32, jnp.bfloat16
PAD = 8
PART = 4
PARTS = 8 // PART
CUTS = 4
ROWS_BEFORE = (5, 10)
ORDER = (3, 13, 11, 5, 4, 12, 2, 14, 10, 6, 1, 15, 9, 7, 8)
LOW, HIGH = -1, 4
SLOTS = HIGH - LOW + 1


def split_bf16(x):
    high = x.astype(BF16)
    return high, (x - high.astype(F32)).astype(BF16)


def kernel(
    nsec, nxs, own, kinds,
    soot, species, kern, split, target, growth, diffusivity, reaction, stoich,
    species_v, soot_v,
    fields, result, dense, rate, used, rate_in, used_in,
    edge_out, edge_in, kern_v, split_v, target_v, growth_v, diff_v, react_v, stoich_s,
    react_pad, weights, lhs,
    load_sem, send_sem, recv_sem, back_send, back_recv, used_send, used_recv, edge_send, edge_recv, ready,
):
    sections = nsec * own
    count = fields.shape[1]
    rows = fields.shape[2]
    blocks = fields.shape[0]
    width = blocks * 128
    me = lax.axis_index("sec")
    at = lax.axis_index("xs")
    before, after = (at + nxs - 1) % nxs, (at + 1) % nxs

    barrier = pltpu.get_barrier_semaphore()
    for step in ORDER:
        pl.semaphore_signal(barrier, inc=1, device_id={"sec": (me + step) % nsec}, device_id_type=MESH)

    @pl.when(at < nxs - 1)
    def _():
        pl.semaphore_signal(barrier, inc=1, device_id={"xs": after}, device_id_type=MESH)


    def tile_rows(p):
        return pl.ds(pl.multiple_of((p // blocks) * 8, 8), 8)

    def part_rows(p, part):
        return pl.ds(pl.multiple_of((p // blocks) * 8 + part * PART, PART), PART)

    def lanes_of(p):
        return pl.ds(pl.multiple_of((p % blocks) * 128, 128), 128)

    loads = [pltpu.make_async_copy(soot.at[:, tile_rows(me), lanes_of(me)], dense.at[pl.ds(PAD + own * me, own)], load_sem.at[0])]
    for b in range(blocks):
        lanes = pl.ds(b * 128, 128)
        loads.append(pltpu.make_async_copy(species.at[:, :, lanes], fields.at[b, pl.ds(0, kinds)], load_sem.at[1 + b]))
        loads.append(pltpu.make_async_copy(soot.at[:, :, lanes], fields.at[b, pl.ds(kinds, own)], load_sem.at[1 + blocks + b]))
    tables = [(kern, kern_v), (split, split_v), (target, target_v), (growth, growth_v), (diffusivity, diff_v), (reaction, react_v), (stoich, stoich_s)]
    for n, (src, dst) in enumerate(tables):
        loads.append(pltpu.make_async_copy(src, dst, load_sem.at[1 + 2 * blocks + n]))
    @pl.when(at == 0)
    def _():
        pl.semaphore_wait(barrier, nsec - 1)

    @pl.when(at > 0)
    def _():
        pl.semaphore_wait(barrier, nsec)
        pl.semaphore_signal(ready, inc=1, device_id={"xs": before}, device_id_type=MESH)

    def cells(p, source, part):
        return pltpu.make_async_remote_copy(
            src_ref=soot.at[:, part_rows(p, part), lanes_of(p)],
            dst_ref=dense.at[pl.ds(PAD + own * source, own), pl.ds(part * PART, PART)],
            send_sem=send_sem.at[part], recv_sem=recv_sem.at[part],
            device_id={"sec": p}, device_id_type=MESH)

    peers = pl.ds(PAD, own * (nsec - 1))

    def all_cells(part):
        piece = dense.at[peers, pl.ds(part * PART, PART)]
        return pltpu.make_async_remote_copy(
            src_ref=piece, dst_ref=piece, send_sem=send_sem.at[part], recv_sem=recv_sem.at[part],
            device_id={"sec": (me + 1) % nsec}, device_id_type=MESH)

    def send_cells(part):
        for step in ORDER:
            cells((me + step) % nsec, me, part).start()

    send_cells(0)
    for copy in loads:
        copy.start()

    zero_tiles = jnp.zeros((PAD, 8, 128), F32)
    dense[0:PAD] = zero_tiles
    dense[PAD + sections:] = zero_tiles
    fields[:, kinds + own:] = jnp.zeros((blocks, count - kinds - own, rows, 128), F32)
    for copy in loads:
        copy.wait()

    flat = fields.reshape(blocks, count * rows, 128)
    flat_result = result.reshape(blocks, count * rows, 128)

    def row_of(r):
        return jnp.concatenate([flat[b, pl.ds(r, count, stride=rows), :] for b in range(blocks)], axis=1)

    edge_out[0] = row_of(0)
    edge_out[1] = row_of(rows - 1)

    def edge(side):
        return pltpu.make_async_remote_copy(
            src_ref=edge_out.at[side], dst_ref=edge_in.at[side],
            send_sem=edge_send.at[side], recv_sem=edge_recv.at[side],
            device_id={"xs": before if side == 0 else after}, device_id_type=MESH)

    @pl.when(at > 0)
    def _():
        edge(0).start()

    @pl.when(at == 0)
    def _():
        edge_in[1] = jnp.zeros((count, width), F32)

    @pl.when(at == nxs - 1)
    def _():
        edge_in[0] = jnp.zeros((count, width), F32)

    i = lax.broadcasted_iota(jnp.int32, (sections, sections), 0)
    j = lax.broadcasted_iota(jnp.int32, (sections, sections), 1)
    rates = kern_v[...]
    shares = split_v[...]
    goal = target_v[...]
    low = 0.5 * rates * shares
    high = 0.5 * rates * (1.0 - shares)
    low_t, high_t, goal_t = low.T, high.T, goal.T
    weights[...] = jnp.zeros(weights.shape, F32)
    for slot in range(SLOTS):
        t = slot + LOW
        lower = jnp.where(goal == i + t, low, 0.0) + jnp.where(goal == i + (t - 1), high, 0.0)
        upper = jnp.where(goal_t == i + t, low_t, 0.0) + jnp.where(goal_t == i + (t - 1), high_t, 0.0)
        value = jnp.where(j <= i, lower, 0.0) + jnp.where(j < i, upper, 0.0)
        if t == 0:
            value = value - rates
        weights[slot, PAD + t:PAD + t + sections, 0:sections] = value
    for slot in range(SLOTS):
        top, rest = split_bf16(weights[slot, PAD:PAD + sections, :])
        here = pl.ds(slot * sections, sections)
        lhs[here, 0:128] = top
        lhs[here, 128:256] = top
        lhs[here, 256:384] = rest
    grow = growth_v[...].reshape(1, sections)
    grow_col = jnp.sum(jnp.where(i == j, grow, 0.0), axis=1, keepdims=True)
    grow_prev = jnp.sum(jnp.where(i == j + 1, grow, 0.0), axis=1, keepdims=True)

    for part in range(1, PARTS):
        send_cells(part)

    fi = lax.broadcasted_iota(jnp.int32, (count, kinds), 0)
    fj = lax.broadcasted_iota(jnp.int32, (count, kinds), 1)
    diff_col = jnp.sum(jnp.where(fi == fj, diff_v[...].reshape(1, kinds), 0.0), axis=1, keepdims=True)
    fc = lax.broadcasted_iota(jnp.int32, (count, 1), 0)
    diff_col = diff_col + jnp.where((fc >= kinds) & (fc < kinds + own), 0.1, 0.0)
    react_pad[...] = jnp.zeros(react_pad.shape, F32)
    react_pad[0:kinds, 0:kinds] = react_v[...]
    mix = react_pad[...]
    mix_top = mix.astype(BF16).astype(F32)
    mix_rest = mix - mix_top
    mix_lhs = (mix_top + pltpu.roll(mix_top, kinds, 1) + pltpu.roll(mix_rest, 2 * kinds, 1)).astype(BF16)
    lane = lax.broadcasted_iota(jnp.int32, (count, width), 1)
    spare = jnp.zeros((128 - 3 * kinds, width), F32)

    def row_step(r, up, down):
        x = row_of(r)
        left = jnp.where(lane == 0, 0.0, pltpu.roll(x, 1, 1))
        right = jnp.where(lane == width - 1, 0.0, pltpu.roll(x, width - 1, 1))
        part = x[0:kinds]
        top = part.astype(BF16).astype(F32)
        rhs = jnp.concatenate([top, part - top, top, spare], axis=0).astype(BF16)
        mixed = jnp.dot(mix_lhs, rhs, preferred_element_type=F32)
        value = x + diff_col * (up + down + left + right - 4.0 * x) + mixed
        for b in range(blocks):
            flat_result[b, pl.ds(r, count, stride=rows), :] = value[:, b * 128:(b + 1) * 128]

    def inner(r, carry):
        row_step(r, row_of(r - 1), row_of(r + 1))
        return carry

    flat_dense = dense.reshape((sections + 2 * PAD) * 8, 128)
    flat_rate = rate.reshape(sections * 8, 128)
    acet = fields[me % blocks, 0, tile_rows(me), :]
    gap = jnp.zeros((128 - sections, 256), BF16)

    def rate_pair(pair):
        r0, r1 = 2 * pair, 2 * pair + 1

        def moved(t):
            start = 8 * (PAD - t)
            return jnp.concatenate(
                [flat_dense[pl.ds(start + r, sections, stride=8), :] for r in (r0, r1)], axis=1)

        held = moved(0)
        top, rest = split_bf16(held)
        rhs = jnp.concatenate([top, gap, rest, gap], axis=0)
        product = jnp.dot(lhs[:, 0:256], rhs, preferred_element_type=F32)
        product = product + jnp.dot(lhs[:, 256:384], rhs[0:128], preferred_element_type=F32)
        total = jnp.zeros((sections, 256), F32)
        for slot in range(SLOTS):
            total = total + moved(slot + LOW) * product[slot * sections:(slot + 1) * sections]
        growing = jnp.concatenate([acet[r0:r0 + 1], acet[r1:r1 + 1]], axis=1)
        flux = grow_col * held * growing
        total = total - flux + grow_prev * moved(1) * growing
        eaten = jnp.sum(flux, axis=0, keepdims=True)
        for n, r in enumerate((r0, r1)):
            flat_rate[pl.ds(r, sections, stride=8), :] = total[:, n * 128:(n + 1) * 128]
            used[r:r + 1, :] = eaten[:, n * 128:(n + 1) * 128]

    def rate_copy(p, source, part):
        return pltpu.make_async_remote_copy(
            src_ref=rate.at[pl.ds(own * p, own), pl.ds(part * PART, PART)],
            dst_ref=rate_in.at[source % blocks, :, part_rows(source, part), :],
            send_sem=back_send.at[part], recv_sem=back_recv.at[part],
            device_id={"sec": p}, device_id_type=MESH)

    def all_rates(part):
        piece = rate.at[pl.ds(0, own * (nsec - 1)), pl.ds(part * PART, PART)]
        return pltpu.make_async_remote_copy(
            src_ref=piece, dst_ref=piece, send_sem=back_send.at[part], recv_sem=back_recv.at[part],
            device_id={"sec": (me + 1) % nsec}, device_id_type=MESH)

    def used_copy(p, part):
        return pltpu.make_async_remote_copy(
            src_ref=used.at[pl.ds(part * PART, PART)], dst_ref=used_in.at[me % blocks, part_rows(me, part), :],
            send_sem=used_send.at[part], recv_sem=used_recv.at[part],
            device_id={"sec": p}, device_id_type=MESH)

    def all_used(part):
        piece = dense.at[pl.ds(PAD, nsec - 1), pl.ds(part * PART, PART)]
        return pltpu.make_async_remote_copy(
            src_ref=piece, dst_ref=piece, send_sem=used_send.at[part], recv_sem=used_recv.at[part],
            device_id={"sec": (me + 1) % nsec}, device_id_type=MESH)

    first = 1
    for part in range(PARTS):
        last = ROWS_BEFORE[part]
        lax.fori_loop(first, last, inner, 0)
        first = last
        all_cells(part).wait_recv()
        for pair in range(part * PART // 2, (part + 1) * PART // 2):
            rate_pair(pair)
        for step in ORDER:
            used_copy((me + step) % nsec, part).start()
        for step in ORDER:
            rate_copy((me + step) % nsec, me, part).start()
        if part == 0:
            @pl.when(at < nxs - 1)
            def _():
                pl.semaphore_wait(ready, 1)
                edge(1).start()
    used_in[me % blocks, tile_rows(me), :] = used[...]
    rate_in[me % blocks, :, tile_rows(me), :] = rate[pl.ds(own * me, own)]

    lax.fori_loop(first, rows - 1, inner, 0)

    @pl.when(at > 0)
    def _():
        edge(0).wait_send()
        edge(1).wait_recv()

    @pl.when(at < nxs - 1)
    def _():
        edge(1).wait_send()
        edge(0).wait_recv()

    row_step(0, edge_in[1], row_of(1))
    row_step(rows - 1, row_of(rows - 2), edge_in[0])

    for part in range(PARTS):
        all_used(part).wait_recv()

    def consume(s, carry):
        for b in range(blocks):
            species_v[s, :, b * 128:(b + 1) * 128] = result[b, s] - stoich_s[s] * used_in[b]
        return carry

    lax.fori_loop(0, kinds, consume, 0)
    for part in range(PARTS):
        all_rates(part).wait_recv()
    for b in range(blocks):
        soot_v[:, :, b * 128:(b + 1) * 128] = result[b, kinds:kinds + own] + rate_in[b]
    for part in range(PARTS):
        all_cells(part).wait_send()
        all_rates(part).wait_send()
    for part in range(PARTS):
        all_used(part).wait_send()


def write_out(species_v, soot_v, species_out, soot_out, sem):
    some = species_v.shape[0] // CUTS
    stores = [
        pltpu.make_async_copy(species_v.at[pl.ds(n * some, some)], species_out.at[pl.ds(n * some, some)], sem.at[n])
        for n in range(CUTS)]
    stores.append(pltpu.make_async_copy(soot_v, soot_out, sem.at[CUTS]))
    for copy in stores:
        copy.start()
    for copy in stores:
        copy.wait()


def stay(x):
    return pltpu.with_memory_space_constraint(x, pltpu.HBM)


def shards(soot, species, kern, split, target, growth, diffusivity, reaction, stoich):
    own, rows, width = soot.shape
    kinds = species.shape[0]
    nsec, nxs = lax.axis_size("sec"), lax.axis_size("xs")
    sections = nsec * own
    blocks = width // 128
    count = -(-(kinds + own) // 8) * 8
    assert blocks * (rows // 8) == nsec and sections <= 128 and 3 * kinds <= 128
    dma = pltpu.SemaphoreType.DMA
    hbm = pl.BlockSpec(memory_space=pltpu.HBM)
    vmem = pl.BlockSpec(memory_space=pltpu.VMEM)
    outs = (jax.ShapeDtypeStruct(species.shape, F32), jax.ShapeDtypeStruct(soot.shape, F32))
    parts = pl.pallas_call(
        functools.partial(kernel, nsec, nxs, own, kinds),
        out_shape=outs,
        in_specs=[hbm] * 9,
        out_specs=(vmem, vmem),
        scratch_shapes=[
            pltpu.VMEM((blocks, count, rows, 128), F32),
            pltpu.VMEM((blocks, count, rows, 128), F32),
            pltpu.VMEM((sections + 2 * PAD, 8, 128), F32),
            pltpu.VMEM((sections, 8, 128), F32),
            pltpu.VMEM((8, 128), F32),
            pltpu.VMEM((blocks, own, rows, 128), F32),
            pltpu.VMEM((blocks, rows, 128), F32),
            pltpu.VMEM((2, count, width), F32),
            pltpu.VMEM((2, count, width), F32),
            pltpu.VMEM(kern.shape, F32),
            pltpu.VMEM(split.shape, F32),
            pltpu.VMEM(target.shape, jnp.int32),
            pltpu.VMEM(growth.shape, F32),
            pltpu.VMEM(diffusivity.shape, F32),
            pltpu.VMEM(reaction.shape, F32),
            pltpu.SMEM(stoich.shape, F32),
            pltpu.VMEM((count, 128), F32),
            pltpu.VMEM((SLOTS, sections + 2 * PAD, 128), F32),
            pltpu.VMEM((SLOTS * sections, 384), BF16),
            dma((1 + 2 * blocks + 7,)),
            *[dma((PARTS,))] * 6,
            dma((2,)), dma((2,)), pltpu.SemaphoreType.REGULAR,
        ],
        compiler_params=pltpu.CompilerParams(
            collective_id=0, has_side_effects=True, vmem_limit_bytes=32 << 20),
    )(*(stay(x) for x in (soot, species, kern, split, target, growth, diffusivity, reaction, stoich)))
    species_out, soot_out = pl.pallas_call(
        write_out,
        out_shape=outs,
        in_specs=[vmem, vmem],
        out_specs=(hbm, hbm),
        scratch_shapes=[dma((CUTS + 1,))],
        compiler_params=pltpu.CompilerParams(vmem_limit_bytes=4 << 20),
    )(*parts)
    return soot_out, species_out


def solution(mesh):
    return jax.shard_map(
        shards,
        mesh=mesh,
        in_specs=(P("sec", "xs", None), P(None, "xs", None), P(), P(), P(), P(), P(), P(), P()),
        out_specs=(P("sec", "xs", None), P(None, "xs", None)),
        check_vma=False,
    )
```

```python
import functools

import jax
import jax.numpy as jnp
from jax import lax
from jax.experimental import pallas as pl
from jax.experimental.pallas import tpu as pltpu
from jax.sharding import PartitionSpec as P

MESH = pl.DeviceIdType.MESH
F32, BF16 = jnp.float32, jnp.bfloat16
PAD = 8
PART = 4
PARTS = 8 // PART
CUTS = 1
ROWS_BEFORE = (5, 10)
ORDER = (3, 13, 11, 5, 4, 12, 2, 14, 10, 6, 1, 15, 9, 7, 8)
LOW, HIGH = -1, 4
SLOTS = HIGH - LOW + 1


def split_bf16(x):
    high = x.astype(BF16)
    return high, (x - high.astype(F32)).astype(BF16)


def kernel(
    nsec, nxs, own, kinds,
    soot, species, kern, split, target, growth, diffusivity, reaction, stoich,
    species_v, soot_v,
    fields, result, dense, rate, used, rate_in, used_in,
    edge_out, edge_in, kern_v, split_v, target_v, growth_v, diff_v, react_v, stoich_s,
    react_pad, weights, lhs,
    load_sem, send_sem, recv_sem, back_send, back_recv, used_send, used_recv, edge_send, edge_recv, ready,
):
    sections = nsec * own
    count = fields.shape[1]
    rows = fields.shape[2]
    blocks = fields.shape[0]
    width = blocks * 128
    me = lax.axis_index("sec")
    at = lax.axis_index("xs")
    before, after = (at + nxs - 1) % nxs, (at + 1) % nxs

    barrier = pltpu.get_barrier_semaphore()
    for step in ORDER:
        pl.semaphore_signal(barrier, inc=1, device_id={"sec": (me + step) % nsec}, device_id_type=MESH)

    @pl.when(at < nxs - 1)
    def _():
        pl.semaphore_signal(barrier, inc=1, device_id={"xs": after}, device_id_type=MESH)


    def tile_rows(p):
        return pl.ds(pl.multiple_of((p // blocks) * 8, 8), 8)

    def part_rows(p, part):
        return pl.ds(pl.multiple_of((p // blocks) * 8 + part * PART, PART), PART)

    def lanes_of(p):
        return pl.ds(pl.multiple_of((p % blocks) * 128, 128), 128)

    loads = [pltpu.make_async_copy(soot.at[:, tile_rows(me), lanes_of(me)], dense.at[pl.ds(PAD + own * me, own)], load_sem.at[0])]
    for b in range(blocks):
        lanes = pl.ds(b * 128, 128)
        loads.append(pltpu.make_async_copy(species.at[:, :, lanes], fields.at[b, pl.ds(0, kinds)], load_sem.at[1 + b]))
        loads.append(pltpu.make_async_copy(soot.at[:, :, lanes], fields.at[b, pl.ds(kinds, own)], load_sem.at[1 + blocks + b]))
    tables = [(kern, kern_v), (split, split_v), (target, target_v), (growth, growth_v), (diffusivity, diff_v), (reaction, react_v), (stoich, stoich_s)]
    for n, (src, dst) in enumerate(tables):
        loads.append(pltpu.make_async_copy(src, dst, load_sem.at[1 + 2 * blocks + n]))
    @pl.when(at == 0)
    def _():
        pl.semaphore_wait(barrier, nsec - 1)

    @pl.when(at > 0)
    def _():
        pl.semaphore_wait(barrier, nsec)
        pl.semaphore_signal(ready, inc=1, device_id={"xs": before}, device_id_type=MESH)

    def cells(p, source, part):
        return pltpu.make_async_remote_copy(
            src_ref=soot.at[:, part_rows(p, part), lanes_of(p)],
            dst_ref=dense.at[pl.ds(PAD + own * source, own), pl.ds(part * PART, PART)],
            send_sem=send_sem.at[part], recv_sem=recv_sem.at[part],
            device_id={"sec": p}, device_id_type=MESH)

    peers = pl.ds(PAD, own * (nsec - 1))

    def all_cells(part):
        piece = dense.at[peers, pl.ds(part * PART, PART)]
        return pltpu.make_async_remote_copy(
            src_ref=piece, dst_ref=piece, send_sem=send_sem.at[part], recv_sem=recv_sem.at[part],
            device_id={"sec": (me + 1) % nsec}, device_id_type=MESH)

    def send_cells(part):
        for step in ORDER:
            cells((me + step) % nsec, me, part).start()

    send_cells(0)
    for copy in loads:
        copy.start()

    zero_tiles = jnp.zeros((PAD, 8, 128), F32)
    dense[0:PAD] = zero_tiles
    dense[PAD + sections:] = zero_tiles
    fields[:, kinds + own:] = jnp.zeros((blocks, count - kinds - own, rows, 128), F32)
    for copy in loads:
        copy.wait()

    flat = fields.reshape(blocks, count * rows, 128)
    flat_result = result.reshape(blocks, count * rows, 128)

    def row_of(r):
        return jnp.concatenate([flat[b, pl.ds(r, count, stride=rows), :] for b in range(blocks)], axis=1)

    edge_out[0] = row_of(0)
    edge_out[1] = row_of(rows - 1)

    def edge(side):
        return pltpu.make_async_remote_copy(
            src_ref=edge_out.at[side], dst_ref=edge_in.at[side],
            send_sem=edge_send.at[side], recv_sem=edge_recv.at[side],
            device_id={"xs": before if side == 0 else after}, device_id_type=MESH)

    @pl.when(at > 0)
    def _():
        edge(0).start()

    @pl.when(at == 0)
    def _():
        edge_in[1] = jnp.zeros((count, width), F32)

    @pl.when(at == nxs - 1)
    def _():
        edge_in[0] = jnp.zeros((count, width), F32)

    i = lax.broadcasted_iota(jnp.int32, (sections, sections), 0)
    j = lax.broadcasted_iota(jnp.int32, (sections, sections), 1)
    rates = kern_v[...]
    shares = split_v[...]
    goal = target_v[...]
    low = 0.5 * rates * shares
    high = 0.5 * rates * (1.0 - shares)
    low_t, high_t, goal_t = low.T, high.T, goal.T
    weights[...] = jnp.zeros(weights.shape, F32)
    for slot in range(SLOTS):
        t = slot + LOW
        lower = jnp.where(goal == i + t, low, 0.0) + jnp.where(goal == i + (t - 1), high, 0.0)
        upper = jnp.where(goal_t == i + t, low_t, 0.0) + jnp.where(goal_t == i + (t - 1), high_t, 0.0)
        value = jnp.where(j <= i, lower, 0.0) + jnp.where(j < i, upper, 0.0)
        if t == 0:
            value = value - rates
        weights[slot, PAD + t:PAD + t + sections, 0:sections] = value
    for slot in range(SLOTS):
        top, rest = split_bf16(weights[slot, PAD:PAD + sections, :])
        here = pl.ds(slot * sections, sections)
        lhs[here, 0:128] = top
        lhs[here, 128:256] = top
        lhs[here, 256:384] = rest
    grow = growth_v[...].reshape(1, sections)
    grow_col = jnp.sum(jnp.where(i == j, grow, 0.0), axis=1, keepdims=True)
    grow_prev = jnp.sum(jnp.where(i == j + 1, grow, 0.0), axis=1, keepdims=True)

    for part in range(1, PARTS):
        send_cells(part)

    fi = lax.broadcasted_iota(jnp.int32, (count, kinds), 0)
    fj = lax.broadcasted_iota(jnp.int32, (count, kinds), 1)
    diff_col = jnp.sum(jnp.where(fi == fj, diff_v[...].reshape(1, kinds), 0.0), axis=1, keepdims=True)
    fc = lax.broadcasted_iota(jnp.int32, (count, 1), 0)
    diff_col = diff_col + jnp.where((fc >= kinds) & (fc < kinds + own), 0.1, 0.0)
    react_pad[...] = jnp.zeros(react_pad.shape, F32)
    react_pad[0:kinds, 0:kinds] = react_v[...]
    mix = react_pad[...]
    mix_top = mix.astype(BF16).astype(F32)
    mix_rest = mix - mix_top
    mix_lhs = (mix_top + pltpu.roll(mix_top, kinds, 1) + pltpu.roll(mix_rest, 2 * kinds, 1)).astype(BF16)
    lane = lax.broadcasted_iota(jnp.int32, (count, width), 1)
    spare = jnp.zeros((128 - 3 * kinds, width), F32)

    def row_step(r, up, down):
        x = row_of(r)
        left = jnp.where(lane == 0, 0.0, pltpu.roll(x, 1, 1))
        right = jnp.where(lane == width - 1, 0.0, pltpu.roll(x, width - 1, 1))
        part = x[0:kinds]
        top = part.astype(BF16).astype(F32)
        rhs = jnp.concatenate([top, part - top, top, spare], axis=0).astype(BF16)
        mixed = jnp.dot(mix_lhs, rhs, preferred_element_type=F32)
        value = x + diff_col * (up + down + left + right - 4.0 * x) + mixed
        for b in range(blocks):
            flat_result[b, pl.ds(r, count, stride=rows), :] = value[:, b * 128:(b + 1) * 128]

    def inner(r, carry):
        row_step(r, row_of(r - 1), row_of(r + 1))
        return carry

    flat_dense = dense.reshape((sections + 2 * PAD) * 8, 128)
    flat_rate = rate.reshape(sections * 8, 128)
    acet = fields[me % blocks, 0, tile_rows(me), :]
    gap = jnp.zeros((128 - sections, 256), BF16)

    def rate_pair(pair):
        r0, r1 = 2 * pair, 2 * pair + 1

        def moved(t):
            start = 8 * (PAD - t)
            return jnp.concatenate(
                [flat_dense[pl.ds(start + r, sections, stride=8), :] for r in (r0, r1)], axis=1)

        held = moved(0)
        top, rest = split_bf16(held)
        rhs = jnp.concatenate([top, gap, rest, gap], axis=0)
        product = jnp.dot(lhs[:, 0:256], rhs, preferred_element_type=F32)
        product = product + jnp.dot(lhs[:, 256:384], rhs[0:128], preferred_element_type=F32)
        total = jnp.zeros((sections, 256), F32)
        for slot in range(SLOTS):
            total = total + moved(slot + LOW) * product[slot * sections:(slot + 1) * sections]
        growing = jnp.concatenate([acet[r0:r0 + 1], acet[r1:r1 + 1]], axis=1)
        flux = grow_col * held * growing
        total = total - flux + grow_prev * moved(1) * growing
        eaten = jnp.sum(flux, axis=0, keepdims=True)
        for n, r in enumerate((r0, r1)):
            flat_rate[pl.ds(r, sections, stride=8), :] = total[:, n * 128:(n + 1) * 128]
            used[r:r + 1, :] = eaten[:, n * 128:(n + 1) * 128]

    def rate_copy(p, source, part):
        return pltpu.make_async_remote_copy(
            src_ref=rate.at[pl.ds(own * p, own), pl.ds(part * PART, PART)],
            dst_ref=rate_in.at[source % blocks, :, part_rows(source, part), :],
            send_sem=back_send.at[part], recv_sem=back_recv.at[part],
            device_id={"sec": p}, device_id_type=MESH)

    def all_rates(part):
        piece = rate.at[pl.ds(0, own * (nsec - 1)), pl.ds(part * PART, PART)]
        return pltpu.make_async_remote_copy(
            src_ref=piece, dst_ref=piece, send_sem=back_send.at[part], recv_sem=back_recv.at[part],
            device_id={"sec": (me + 1) % nsec}, device_id_type=MESH)

    def used_copy(p, part):
        return pltpu.make_async_remote_copy(
            src_ref=used.at[pl.ds(part * PART, PART)], dst_ref=used_in.at[me % blocks, part_rows(me, part), :],
            send_sem=used_send.at[part], recv_sem=used_recv.at[part],
            device_id={"sec": p}, device_id_type=MESH)

    def all_used(part):
        piece = dense.at[pl.ds(PAD, nsec - 1), pl.ds(part * PART, PART)]
        return pltpu.make_async_remote_copy(
            src_ref=piece, dst_ref=piece, send_sem=used_send.at[part], recv_sem=used_recv.at[part],
            device_id={"sec": (me + 1) % nsec}, device_id_type=MESH)

    first = 1
    for part in range(PARTS):
        last = ROWS_BEFORE[part]
        lax.fori_loop(first, last, inner, 0)
        first = last
        all_cells(part).wait_recv()
        for pair in range(part * PART // 2, (part + 1) * PART // 2):
            rate_pair(pair)
        if part == PARTS - 1:
            for step in ORDER:
                used_copy((me + step) % nsec, part).start()
        for step in ORDER:
            rate_copy((me + step) % nsec, me, part).start()
        if part < PARTS - 1:
            for step in ORDER:
                used_copy((me + step) % nsec, part).start()
        if part == 0:
            @pl.when(at < nxs - 1)
            def _():
                pl.semaphore_wait(ready, 1)
                edge(1).start()
    used_in[me % blocks, tile_rows(me), :] = used[...]
    rate_in[me % blocks, :, tile_rows(me), :] = rate[pl.ds(own * me, own)]

    lax.fori_loop(first, rows - 1, inner, 0)

    @pl.when(at > 0)
    def _():
        edge(0).wait_send()
        edge(1).wait_recv()

    @pl.when(at < nxs - 1)
    def _():
        edge(1).wait_send()
        edge(0).wait_recv()

    row_step(0, edge_in[1], row_of(1))
    row_step(rows - 1, row_of(rows - 2), edge_in[0])

    for part in range(PARTS):
        all_used(part).wait_recv()

    def consume(s, carry):
        for b in range(blocks):
            species_v[s, :, b * 128:(b + 1) * 128] = result[b, s] - stoich_s[s] * used_in[b]
        return carry

    lax.fori_loop(0, kinds, consume, 0)
    for part in range(PARTS):
        all_rates(part).wait_recv()
    for b in range(blocks):
        soot_v[:, :, b * 128:(b + 1) * 128] = result[b, kinds:kinds + own] + rate_in[b]
    for part in range(PARTS):
        all_cells(part).wait_send()
        all_rates(part).wait_send()
    for part in range(PARTS):
        all_used(part).wait_send()


def write_out(species_v, soot_v, species_out, soot_out, sem):
    some = species_v.shape[0] // CUTS
    stores = [
        pltpu.make_async_copy(species_v.at[pl.ds(n * some, some)], species_out.at[pl.ds(n * some, some)], sem.at[n])
        for n in range(CUTS)]
    stores.append(pltpu.make_async_copy(soot_v, soot_out, sem.at[CUTS]))
    for copy in stores:
        copy.start()
    for copy in stores:
        copy.wait()


def stay(x):
    return pltpu.with_memory_space_constraint(x, pltpu.HBM)


def shards(soot, species, kern, split, target, growth, diffusivity, reaction, stoich):
    own, rows, width = soot.shape
    kinds = species.shape[0]
    nsec, nxs = lax.axis_size("sec"), lax.axis_size("xs")
    sections = nsec * own
    blocks = width // 128
    count = -(-(kinds + own) // 8) * 8
    assert blocks * (rows // 8) == nsec and sections <= 128 and 3 * kinds <= 128
    dma = pltpu.SemaphoreType.DMA
    hbm = pl.BlockSpec(memory_space=pltpu.HBM)
    vmem = pl.BlockSpec(memory_space=pltpu.VMEM)
    outs = (jax.ShapeDtypeStruct(species.shape, F32), jax.ShapeDtypeStruct(soot.shape, F32))
    parts = pl.pallas_call(
        functools.partial(kernel, nsec, nxs, own, kinds),
        out_shape=outs,
        in_specs=[hbm] * 9,
        out_specs=(vmem, vmem),
        scratch_shapes=[
            pltpu.VMEM((blocks, count, rows, 128), F32),
            pltpu.VMEM((blocks, count, rows, 128), F32),
            pltpu.VMEM((sections + 2 * PAD, 8, 128), F32),
            pltpu.VMEM((sections, 8, 128), F32),
            pltpu.VMEM((8, 128), F32),
            pltpu.VMEM((blocks, own, rows, 128), F32),
            pltpu.VMEM((blocks, rows, 128), F32),
            pltpu.VMEM((2, count, width), F32),
            pltpu.VMEM((2, count, width), F32),
            pltpu.VMEM(kern.shape, F32),
            pltpu.VMEM(split.shape, F32),
            pltpu.VMEM(target.shape, jnp.int32),
            pltpu.VMEM(growth.shape, F32),
            pltpu.VMEM(diffusivity.shape, F32),
            pltpu.VMEM(reaction.shape, F32),
            pltpu.SMEM(stoich.shape, F32),
            pltpu.VMEM((count, 128), F32),
            pltpu.VMEM((SLOTS, sections + 2 * PAD, 128), F32),
            pltpu.VMEM((SLOTS * sections, 384), BF16),
            dma((1 + 2 * blocks + 7,)),
            *[dma((PARTS,))] * 6,
            dma((2,)), dma((2,)), pltpu.SemaphoreType.REGULAR,
        ],
        compiler_params=pltpu.CompilerParams(
            collective_id=0, has_side_effects=True, vmem_limit_bytes=32 << 20),
    )(*(stay(x) for x in (soot, species, kern, split, target, growth, diffusivity, reaction, stoich)))
    species_out, soot_out = pl.pallas_call(
        write_out,
        out_shape=outs,
        in_specs=[vmem, vmem],
        out_specs=(hbm, hbm),
        scratch_shapes=[dma((CUTS + 1,))],
        compiler_params=pltpu.CompilerParams(vmem_limit_bytes=4 << 20),
    )(*parts)
    return soot_out, species_out


def solution(mesh):
    return jax.shard_map(
        shards,
        mesh=mesh,
        in_specs=(P("sec", "xs", None), P(None, "xs", None), P(), P(), P(), P(), P(), P(), P()),
        out_specs=(P("sec", "xs", None), P(None, "xs", None)),
        check_vma=False,
    )
```
